32 devices in a mesh: groups: 2 (over y), seq: 4 (over z), role: 4 (over x, core).
Axes of the slice: x: 2, y: 2, z: 4, core: 2. Of those that a mesh axis runs over, the one named last changes fastest.
Arguments:
- queries: bfloat16 [8, 512, 4096], P(('groups', 'role'), 'seq'), parts along dimension 0, may hold values from -500 to 500
- keys: bfloat16 [8, 512, 4096], P(('groups', 'role'), 'seq'), parts along dimension 0, may hold values from -500 to 500
- values: bfloat16 [8, 512, 4096], P(('groups', 'role'), 'seq'), parts along dimension 0, may hold values from -6 to 6
- q_gain: float32 [4096], replicated, may hold values from 1.2 to 1.8
- k_gain: float32 [4096], replicated, may hold values from 1.2 to 1.8
- latent_frames: bfloat16 [8, 8, 160, 384], P(('groups', 'role'), 'seq'), parts along dimension 0, may hold values from -6 to 6
- frame_cache: bfloat16 [4, 8, 160, 384], P('groups', 'seq'), parts along dimension 0, may hold values from -6 to 6
- vae_gain: float32 [384], replicated, may hold values from 0.5 to 1.5
- conv_weight: bfloat16 [3, 3, 3, 384, 384], replicated, may hold values from -0.0625 to 0.0625
- conv_bias: float32 [384], replicated, may hold values from -1.5 to 1.5
Outputs:
- attended: bfloat16 [8, 512, 4096], P(('groups', 'role'), 'seq'), parts along dimension 0
- decoded: bfloat16 [8, 8, 160, 384], P(('groups', 'role'), 'seq'), parts along dimension 0
The draws below stay inside these ranges and needn't reach their ends.
There are 2 independent parts, one for each index of `groups`. The reference program is written for one: setup_inputs(seed, part) draws one part's arguments, and reference() takes and returns one part's arrays. A program takes and returns all parts, laid end to end along the dimension named above; an argument that names none is the same for every part. Nothing has to cross between parts.
All inputs are finite; a program needn't handle non-finite values.
Results may differ from the reference program's by a relative error of at most 0.0025.
The reference program's roundings to bfloat16 on the way count: a program that leaves them out, or rounds other values in their place, can miss the bound.
Values may be sent and summed in bfloat16 or wider, within the bound.
No kernel may reach another device: no remote copies, remote signals or barrier semaphores. Data moves between devices by JAX's collectives and lax.ppermute only.
A program may use at most 128 MiB of HBM per device.

```python
import math
import jax
import jax.numpy as jnp
from jax import lax

HEADS = 32
HEAD_DIM = 128
CHANNELS = 384
COLS = 160
TOKENS = 512
SAMPLES = 4
FRAMES = 4
ROWS = 8


def scaled_normal(key):
    width = HEADS * HEAD_DIM
    base = jnp.clip(jax.random.normal(jax.random.fold_in(key, 1), (SAMPLES, TOKENS, width), jnp.float32), -5.0, 5.0)
    row_scale = jnp.exp(jax.random.uniform(jax.random.fold_in(key, 2), (SAMPLES, TOKENS, 1), jnp.float32, 0.0, jnp.log(10.0)))
    col_scale = jnp.exp(jax.random.uniform(jax.random.fold_in(key, 3), (1, 1, width), jnp.float32, 0.0, jnp.log(10.0)))
    return base * row_scale * col_scale


def draw_queries(key, part):
    result = scaled_normal(jax.random.fold_in(key, 11))
    return result.astype(jnp.bfloat16)


def draw_keys(key, part):
    result = scaled_normal(jax.random.fold_in(key, 12))
    return result.astype(jnp.bfloat16)


def shard_levels(own_key, shape, cuts, least, top_value):
    level = 1.0
    for dim, parts in cuts:
        heights = jax.random.uniform(jax.random.fold_in(jax.random.fold_in(own_key, 6), dim), (parts,), jnp.float32, least / len(cuts), top_value / len(cuts))
        level = level * jnp.repeat(jnp.exp(heights), shape[dim] // parts).reshape((-1,) + (1,) * (len(shape) - 1 - dim))
    return level


def centred(own_key, extent, deviation, reach, cuts=(), kind=jnp.bfloat16):
    entries = deviation * jax.random.normal(own_key, extent, jnp.float32)
    if cuts:
        entries = entries * shard_levels(own_key, extent, cuts, -0.22, 0.18)
    return jnp.clip(entries, -reach, reach).astype(kind)


def setup_inputs(seed: int = 0, part: int = 0) -> dict:
    streams_of = jax.random.split(jax.random.key(seed), 11)
    part_splits = jax.random.split(jax.random.fold_in(streams_of[10], part), 11)
    queries = draw_queries(jax.random.fold_in(jax.random.fold_in(streams_of[10], part), 71), part)
    keys = draw_keys(jax.random.fold_in(jax.random.fold_in(streams_of[10], part), 71), part)
    values = centred(part_splits[2], (SAMPLES, TOKENS, HEADS * HEAD_DIM), 1.0, 6.0, ((0, 4), (1, 4)))
    q_gain = jnp.clip(jnp.exp(jax.random.uniform(streams_of[3], (HEADS * HEAD_DIM,), jnp.float32, math.log(1.2), math.log(1.8))), 1.2, 1.8)
    k_gain = jnp.clip(jnp.exp(jax.random.uniform(streams_of[4], (HEADS * HEAD_DIM,), jnp.float32, math.log(1.2), math.log(1.8))), 1.2, 1.8)
    latent_frames = centred(part_splits[5], (FRAMES, ROWS, COLS, CHANNELS), 1.0, 6.0, ((0, 4), (1, 4)))
    frame_cache = centred(part_splits[6], (2, ROWS, COLS, CHANNELS), 1.0, 6.0, ((1, 4),))
    vae_gain = jnp.clip(1.0 + 0.1 * jax.random.normal(streams_of[7], (CHANNELS,), jnp.float32), 0.5, 1.5)
    conv_weight = centred(streams_of[8], (3, 3, 3, CHANNELS, CHANNELS), (27 * CHANNELS) ** -0.5, 0.0625)
    conv_bias = centred(streams_of[9], (CHANNELS,), 0.3, 1.5, (), jnp.float32)
    return dict(queries=queries, keys=keys, values=values, q_gain=q_gain, k_gain=k_gain, latent_frames=latent_frames, frame_cache=frame_cache, vae_gain=vae_gain, conv_weight=conv_weight, conv_bias=conv_bias)


EPSILON = 1e-06

def rms_scale(rows, gain):
    values_f = rows.astype(jnp.float32)
    mean_sq = lax.optimization_barrier(jnp.mean(values_f * values_f, axis=-1, keepdims=True))
    return values_f * lax.rsqrt(mean_sq + EPSILON) * gain.astype(jnp.float32)

def head_attention(triple):
    q_head, k_head, v_head = triple
    length = q_head.shape[0]
    block = min(512, length)
    scale = q_head.shape[1] ** (-0.5)
    k_wide = k_head.astype(jnp.float32)
    v_wide = v_head.astype(jnp.float32)

    def one_block(start):
        rows = lax.dynamic_slice_in_dim(q_head, start, block, 0).astype(jnp.float32)
        scores = jnp.einsum('qd,kd->qk', rows, k_wide, precision=lax.Precision.HIGHEST) * scale
        top = lax.optimization_barrier(jnp.max(scores, axis=1, keepdims=True))
        weights = jnp.exp(scores - top)
        total = lax.optimization_barrier(jnp.sum(weights, axis=1, keepdims=True))
        rounded = weights.astype(jnp.bfloat16).astype(jnp.float32)
        mixed = jnp.dot(rounded, v_wide, precision=lax.Precision.HIGHEST) / total
        return mixed.astype(jnp.bfloat16)
    starts = jnp.arange(length // block, dtype=jnp.int32) * block
    return lax.map(one_block, starts).reshape(length, -1)

def reference(queries, keys, values, q_gain, k_gain, latent_frames, frame_cache, vae_gain, conv_weight, conv_bias):
    samples, tokens, width = queries.shape
    heads = HEADS
    depth = width // heads
    q_normed = rms_scale(queries, q_gain).astype(jnp.bfloat16)
    k_normed = rms_scale(keys, k_gain).astype(jnp.bfloat16)

    def by_head(array):
        return jnp.transpose(array.reshape(samples, tokens, heads, depth), (0, 2, 1, 3)).reshape(samples * heads, tokens, depth)
    outputs = lax.map(head_attention, (by_head(q_normed), by_head(k_normed), by_head(values)))
    attended = jnp.transpose(outputs.reshape(samples, heads, tokens, depth), (0, 2, 1, 3)).reshape(samples, tokens, width)
    joined = jnp.concatenate([frame_cache, latent_frames], axis=0)
    activated = jax.nn.silu(rms_scale(joined, vae_gain)).astype(jnp.bfloat16)
    padded = jnp.pad(activated, ((0, 0), (1, 1), (1, 1), (0, 0)))
    rows = latent_frames.shape[1]
    cols = latent_frames.shape[2]
    chans = latent_frames.shape[3]
    weight = conv_weight.reshape(27 * chans, chans).astype(jnp.float32)

    def one_frame(index):
        window = lax.dynamic_slice_in_dim(padded, index, 3, 0)
        pieces = []
        for a in range(3):
            for b in range(3):
                for e in range(3):
                    pieces.append(window[a, b:b + rows, e:e + cols, :])
        columns = jnp.concatenate(pieces, axis=-1).reshape(rows * cols, 27 * chans).astype(jnp.float32)
        return jnp.dot(columns, weight, precision=lax.Precision.HIGHEST).reshape(rows, cols, chans)
    conv = lax.map(one_frame, jnp.arange(latent_frames.shape[0], dtype=jnp.int32))
    decoded = (latent_frames.astype(jnp.float32) + conv + conv_bias).astype(jnp.bfloat16)
    return (attended, decoded)
```

```python
import functools

import jax
import jax.numpy as jnp
from jax import lax
from jax.experimental import pallas as pl
from jax.experimental.pallas import tpu as pltpu
from jax.sharding import PartitionSpec as P

HEAD_DIM = 128
EPSILON = 1e-06
CHUNK_HEADS = 4


def swap(value, axis, mask):
    count = lax.axis_size(axis)
    return lax.ppermute(value, axis, [(i, i ^ mask) for i in range(count)])


def shift(value, axis, steps):
    count = lax.axis_size(axis)
    return lax.ppermute(
        value, axis, [(i, i + steps) for i in range(count) if 0 <= i + steps < count]
    )


def around(value, axis, steps):
    count = lax.axis_size(axis)
    return lax.ppermute(value, axis, [(i, (i + steps) % count) for i in range(count)])


def pack_kernel(half, chunks, wide, place_ref, q_ref, k_ref, v_ref, qg_ref, kg_ref, *outs):
    place = lax.rem(place_ref[0], half)

    def scale_of(ref):
        rows = ref[...].astype(jnp.float32)
        return lax.rsqrt(jnp.mean(rows * rows, axis=-1, keepdims=True) + EPSILON)

    q_scale = scale_of(q_ref)
    k_scale = scale_of(k_ref)
    class_wide = chunks * wide
    outs = list(outs)
    for chunk in range(chunks):
        for mask in range(half):
            start = pl.multiple_of((place ^ mask) * class_wide + chunk * wide, 128)
            cols = pl.ds(start, wide)
            q_part = q_ref[:, cols].astype(jnp.float32) * q_scale * qg_ref[:, cols]
            k_part = k_ref[:, cols].astype(jnp.float32) * k_scale * kg_ref[:, cols]
            q_part = q_part.astype(jnp.bfloat16)
            k_part = k_part.astype(jnp.bfloat16)
            v_part = v_ref[:, cols]
            if mask == 0:
                outs.pop(0)[...] = q_part
                pair = outs.pop(0)
                pair[0] = k_part
                pair[1] = v_part
            else:
                near = outs.pop(0)
                near[0] = q_part
                near[1] = k_part
                near[2] = v_part
                far = outs.pop(0)
                far[0] = k_part
                far[1] = v_part


def pack(place, queries, keys, values, q_gain, k_gain, half, chunks, wide):
    tokens, width = queries.shape
    rows = min(tokens, 32)
    bf16 = jnp.bfloat16
    shapes, specs = [], []

    def add(count):
        if count:
            shapes.append(jax.ShapeDtypeStruct((count, tokens, wide), bf16))
            specs.append(pl.BlockSpec((count, rows, wide), lambda i, *_: (0, i, 0)))
        else:
            shapes.append(jax.ShapeDtypeStruct((tokens, wide), bf16))
            specs.append(pl.BlockSpec((rows, wide), lambda i, *_: (i, 0)))

    for _ in range(chunks):
        add(0)
        add(2)
        for _ in range(1, half):
            add(3)
            add(2)
    token_spec = pl.BlockSpec((rows, width), lambda i, *_: (i, 0))
    gain_spec = pl.BlockSpec((1, width), lambda i, *_: (0, 0))
    outs = pl.pallas_call(
        functools.partial(pack_kernel, half, chunks, wide),
        grid_spec=pltpu.PrefetchScalarGridSpec(
            num_scalar_prefetch=1,
            grid=(tokens // rows,),
            in_specs=[token_spec] * 3 + [gain_spec] * 2,
            out_specs=specs,
        ),
        out_shape=shapes,
        name="pack",
    )(place, queries, keys, values, q_gain[None], k_gain[None])
    outs = list(outs)
    result = []
    for _ in range(chunks):
        own_q, own_kv = outs.pop(0), outs.pop(0)
        near, far = [], []
        for _ in range(1, half):
            near.append(outs.pop(0))
            far.append(outs.pop(0))
        result.append((own_q, own_kv, near, far))
    return result


def attend_kernel(half, group, own_q, own_kv, *refs):
    near = refs[: half - 1]
    far = refs[half - 1 : 2 * half - 1]
    outs = refs[2 * half - 1 :]
    scale = own_q.shape[-1] ** (-0.5)
    k_all = jnp.concatenate(
        [own_kv[0]] + [ref[1] for ref in near] + [ref[0] for ref in far], axis=0
    )
    v_all = jnp.concatenate(
        [own_kv[1]] + [ref[2] for ref in near] + [ref[1] for ref in far], axis=0
    )
    tokens = own_q.shape[0]
    blocks = [own_q[...]] + [ref[0] for ref in near]
    for first in range(0, half, group):
        part = blocks[first : first + group]
        rows = jnp.concatenate(part, axis=0) if len(part) > 1 else part[0]
        scores = (
            lax.dot_general(
                rows, k_all, (((1,), (1,)), ((), ())), preferred_element_type=jnp.float32
            )
            * scale
        )
        top = jnp.max(scores, axis=1, keepdims=True)
        weights = jnp.exp(scores - top)
        total = jnp.sum(weights, axis=1, keepdims=True)
        mixed = (
            jnp.dot(weights.astype(jnp.bfloat16), v_all, preferred_element_type=jnp.float32)
            / total
        )
        mixed = mixed.astype(jnp.bfloat16)
        for i in range(len(part)):
            outs[first + i][...] = mixed[i * tokens : (i + 1) * tokens]


def attend(own_q, own_kv, near, far):
    tokens, wide = own_q.shape
    half = len(near) + 1
    keys = 2 * half * tokens
    group = max(1, min(half, (256 * 1024) // (keys * tokens)))
    flat = pl.BlockSpec((tokens, HEAD_DIM), lambda h: (0, h))

    def stack(count):
        return pl.BlockSpec((count, tokens, HEAD_DIM), lambda h: (0, 0, h))

    heads = wide // HEAD_DIM
    return pl.pallas_call(
        functools.partial(attend_kernel, half, group),
        grid=(heads,),
        in_specs=[flat, stack(2)] + [stack(3)] * (half - 1) + [stack(2)] * half,
        out_specs=[flat] * half,
        out_shape=[jax.ShapeDtypeStruct((tokens, wide), jnp.bfloat16)] * half,
        cost_estimate=pl.CostEstimate(
            flops=4 * heads * half * tokens * keys * HEAD_DIM,
            transcendentals=heads * half * tokens * keys,
            bytes_accessed=2 * heads * HEAD_DIM * (2 * half * tokens + 2 * keys),
        ),
        name="attend",
    )(own_q, own_kv, *near, *far)


def join_kernel(half, chunks, wide, place_ref, *refs):
    out = refs[-1]
    place = lax.rem(place_ref[0], half)
    for chunk in range(chunks):
        for mask in range(half):
            start = pl.multiple_of((place ^ mask) * chunks * wide + chunk * wide, 128)
            out[:, pl.ds(start, wide)] = refs[chunk * half + mask][...]


def join(place, pieces, half, chunks, wide):
    tokens = pieces[0].shape[0]
    whole = pl.BlockSpec(memory_space=pltpu.VMEM)
    return pl.pallas_call(
        functools.partial(join_kernel, half, chunks, wide),
        in_specs=[pl.BlockSpec(memory_space=pltpu.SMEM)] + [whole] * len(pieces),
        out_specs=whole,
        out_shape=jax.ShapeDtypeStruct((tokens, half * chunks * wide), jnp.bfloat16),
        name="join",
    )(place, *pieces)


def conv_kernel(own_ref, one_ref, two_ref, weight_ref, latent_ref, bias_ref, out_ref, acc_ref):
    step = pl.program_id(0)
    rows, cols, chans = latent_ref.shape

    def add(frame_ref):
        for e in range(3):
            total = None
            for b in range(3):
                cells = frame_ref[b : b + rows].reshape(rows * cols, chans)
                part = jnp.dot(cells, weight_ref[0, b, e], preferred_element_type=jnp.float32)
                total = part if total is None else total + part

            @pl.when(step == 0)
            def _():
                acc_ref[e] = total

            @pl.when(step > 0)
            def _():
                acc_ref[e] += total

    @pl.when(step == 0)
    def _():
        add(two_ref)

    @pl.when(step == 1)
    def _():
        add(one_ref)

    @pl.when(step == 2)
    def _():
        add(own_ref)
        line = jnp.zeros((1, chans), jnp.float32)
        for row in range(rows):
            cells = pl.ds(row * cols, cols)
            left = jnp.concatenate([line, acc_ref[0, cells][: cols - 1]], axis=0)
            right = jnp.concatenate([acc_ref[2, cells][1:], line], axis=0)
            conv = left + acc_ref[1, cells] + right
            out_ref[row] = (
                latent_ref[row].astype(jnp.float32) + conv + bias_ref[...]
            ).astype(jnp.bfloat16)


def convolve(own, one_back, two_back, weight, latent, bias):
    rows, cols, chans = latent.shape
    frame = pl.BlockSpec(own.shape, lambda a: (0, 0, 0))
    image = pl.BlockSpec(latent.shape, lambda a: (0, 0, 0))
    return pl.pallas_call(
        conv_kernel,
        grid=(3,),
        in_specs=[
            frame,
            frame,
            frame,
            pl.BlockSpec((1,) + weight.shape[1:], lambda a: (a, 0, 0, 0, 0)),
            image,
            pl.BlockSpec((1, chans), lambda a: (0, 0)),
        ],
        out_specs=image,
        out_shape=jax.ShapeDtypeStruct(latent.shape, jnp.bfloat16),
        scratch_shapes=[pltpu.VMEM((3, rows * cols, chans), jnp.float32)],
        cost_estimate=pl.CostEstimate(
            flops=2 * 27 * rows * cols * chans * chans,
            transcendentals=0,
            bytes_accessed=2 * 27 * chans * chans,
        ),
        name="convolve",
    )(own, one_back, two_back, weight, latent, bias[None])


def activate_kernel(latent_ref, cache_ref, gain_ref, own_ref, past_ref):
    def act(rows):
        rows = rows.astype(jnp.float32)
        mean_sq = jnp.mean(rows * rows, axis=-1, keepdims=True)
        return jax.nn.silu(rows * lax.rsqrt(mean_sq + EPSILON) * gain_ref[...]).astype(
            jnp.bfloat16
        )

    own_ref[...] = act(latent_ref[...])
    past_ref[...] = act(cache_ref[...])


def activate(latent, cache, gain):
    whole = pl.BlockSpec(memory_space=pltpu.VMEM)
    return pl.pallas_call(
        activate_kernel,
        in_specs=[whole] * 3,
        out_specs=[whole] * 2,
        out_shape=[
            jax.ShapeDtypeStruct(latent.shape, jnp.bfloat16),
            jax.ShapeDtypeStruct(cache.shape, jnp.bfloat16),
        ],
        name="activate",
    )(latent, cache, gain[None])


def decode(latent_frames, frame_cache, vae_gain, conv_weight, conv_bias):
    place = lax.axis_index("role")
    latent = latent_frames[0]
    chosen = jnp.where(place == 0, frame_cache[0], frame_cache[1])
    own, past = activate(latent, chosen, vae_gain)
    below = shift(jnp.stack([own[-1], past[-1]]), "seq", 1)
    above = shift(jnp.stack([own[0], past[0]]), "seq", -1)
    own = jnp.concatenate([below[:1], own, above[:1]], axis=0)
    past = jnp.concatenate([below[1:], past, above[1:]], axis=0)
    outgoing = jnp.where(place == lax.axis_size("role") - 1, past, own)
    one_back = around(outgoing, "role", 1)
    two_back = jnp.where(place == 0, past, around(outgoing, "role", 2))
    return convolve(own, one_back, two_back, conv_weight, latent, conv_bias)[None]


def body(
    queries,
    keys,
    values,
    q_gain,
    k_gain,
    latent_frames,
    frame_cache,
    vae_gain,
    conv_weight,
    conv_bias,
):
    width = queries.shape[2]
    ring = lax.axis_size("seq")
    half = ring // 2
    class_heads = width // HEAD_DIM // half
    chunks = max(1, class_heads // CHUNK_HEADS)
    wide = class_heads // chunks * HEAD_DIM
    place = lax.axis_index("seq").astype(jnp.int32)[None]
    packed = pack(
        place, queries[0], keys[0], values[0], q_gain, k_gain, half, chunks, wide
    )
    pieces = []
    for own_q, own_kv, near, far in packed:
        near_in = [swap(near[mask - 1], "seq", mask) for mask in range(1, half)]
        far_in = [swap(own_kv, "seq", half)]
        far_in += [swap(far[mask - 1], "seq", half + mask) for mask in range(1, half)]
        mixed = attend(own_q, own_kv, near_in, far_in)
        pieces.append(mixed[0])
        pieces += [swap(mixed[mask], "seq", mask) for mask in range(1, half)]
    decoded = decode(latent_frames, frame_cache, vae_gain, conv_weight, conv_bias)
    attended = join(place, pieces, half, chunks, wide)[None]
    return (attended, decoded)


def solution(mesh):
    return jax.shard_map(
        body,
        mesh=mesh,
        in_specs=(
            P(("groups", "role"), "seq", None),
            P(("groups", "role"), "seq", None),
            P(("groups", "role"), "seq", None),
            P(),
            P(),
            P(("groups", "role"), "seq", None, None),
            P("groups", "seq", None, None),
            P(),
            P(),
            P(),
        ),
        out_specs=(P(("groups", "role"), "seq", None), P(("groups", "role"), "seq", None, None)),
        check_vma=False,
    )
```

```python
import functools

import jax
import jax.numpy as jnp
from jax import lax
from jax.experimental import pallas as pl
from jax.experimental.pallas import tpu as pltpu
from jax.sharding import PartitionSpec as P


HEAD_DIM = 128
EPSILON = 1e-06


def swap(value, axis, mask):
    count = lax.axis_size(axis)
    return lax.ppermute(value, axis, [(i, i ^ mask) for i in range(count)])


def shift(value, axis, steps):
    count = lax.axis_size(axis)
    return lax.ppermute(
        value, axis, [(i, i + steps) for i in range(count) if 0 <= i + steps < count]
    )


def around(value, axis, steps):
    count = lax.axis_size(axis)
    return lax.ppermute(value, axis, [(i, (i + steps) % count) for i in range(count)])


def in_hbm(array):
    return pltpu.with_memory_space_constraint(array, pltpu.HBM)


def chunks_of(heads):
    if heads % 8:
        return [heads]
    return [heads // 4] * 3 + [heads // 8] * 2


def split_kernel(half, parts, place_ref, v_ref, *refs):
    outs, sems = refs[:-1], refs[-1]
    place = lax.rem(place_ref[0], half)
    class_wide = sum(parts)
    copies = []
    first = 0
    for part, wide in enumerate(parts):
        for mask in range(half):
            start = pl.multiple_of((place ^ mask) * class_wide + first, HEAD_DIM)
            index = part * half + mask
            copies.append(
                pltpu.make_async_copy(
                    v_ref.at[:, pl.ds(start, wide)], outs[index], sems.at[index]
                )
            )
        first += wide
    for copy in copies:
        copy.start()
    for copy in copies:
        copy.wait()


def split(place, values, half, parts):
    tokens = values.shape[0]
    anywhere = pl.BlockSpec(memory_space=pl.ANY)
    outs = pl.pallas_call(
        functools.partial(split_kernel, half, parts),
        in_specs=[pl.BlockSpec(memory_space=pltpu.SMEM), anywhere],
        out_specs=[anywhere] * (half * len(parts)),
        out_shape=[
            jax.ShapeDtypeStruct((tokens, wide), values.dtype)
            for wide in parts
            for _ in range(half)
        ],
        scratch_shapes=[pltpu.SemaphoreType.DMA((half * len(parts),))],
        name="split",
    )(place, values)
    return [outs[i * half : (i + 1) * half] for i in range(len(parts))]


def pack_kernel(half, sizes, place_ref, q_ref, k_ref, qg_ref, kg_ref, after_ref, *outs):
    place = lax.rem(place_ref[0], half)

    def scale_of(ref):
        rows = ref[...].astype(jnp.float32)
        return lax.rsqrt(jnp.mean(rows * rows, axis=-1, keepdims=True) + EPSILON)

    q_scale = scale_of(q_ref)
    k_scale = scale_of(k_ref)
    class_wide = sum(sizes)
    outs = list(outs)
    first = 0
    for wide in sizes:
        for mask in range(half):
            start = pl.multiple_of((place ^ mask) * class_wide + first, HEAD_DIM)
            cols = pl.ds(start, wide)
            q_part = q_ref[:, cols].astype(jnp.float32) * q_scale * qg_ref[:, cols]
            k_part = k_ref[:, cols].astype(jnp.float32) * k_scale * kg_ref[:, cols]
            q_part = q_part.astype(jnp.bfloat16)
            k_part = k_part.astype(jnp.bfloat16)
            if mask == 0:
                outs.pop(0)[...] = q_part
                outs.pop(0)[...] = k_part
            else:
                near = outs.pop(0)
                near[0] = q_part
                near[1] = k_part
                outs.pop(0)[...] = k_part
        first += wide


def pack(place, queries, keys, q_gain, k_gain, after, half, sizes):
    tokens, width = queries.shape
    rows = min(tokens, 32)
    shapes, specs = [], []

    def add(wide, *lead):
        shapes.append(jax.ShapeDtypeStruct(lead + (tokens, wide), jnp.bfloat16))
        specs.append(
            pl.BlockSpec(lead + (rows, wide), lambda i, *_: (0,) * len(lead) + (i, 0))
        )

    for wide in sizes:
        add(wide)
        add(wide)
        for _ in range(1, half):
            add(wide, 2)
            add(wide)
    token_spec = pl.BlockSpec((rows, width), lambda i, *_: (i, 0))
    gain_spec = pl.BlockSpec((1, width), lambda i, *_: (0, 0))
    outs = pl.pallas_call(
        functools.partial(pack_kernel, half, sizes),
        grid_spec=pltpu.PrefetchScalarGridSpec(
            num_scalar_prefetch=1,
            grid=(tokens // rows,),
            in_specs=[token_spec] * 2
            + [gain_spec] * 2
            + [pl.BlockSpec(memory_space=pl.ANY)],
            out_specs=specs,
        ),
        out_shape=shapes,
        name="pack",
    )(place, queries, keys, q_gain[None], k_gain[None], after)
    outs = list(outs)
    result = []
    for _ in sizes:
        own_q, own_k = outs.pop(0), outs.pop(0)
        near, far = [], []
        for _ in range(1, half):
            near.append(outs.pop(0))
            far.append(outs.pop(0))
        result.append((own_q, own_k, near, far))
    return result


def attend_kernel(half, group, extra, place_ref, *refs):
    own_q, own_k, own_v = refs[:3]
    near = refs[3 : half + 2]
    far = refs[half + 2 : 2 * half + 2]
    near_v = refs[2 * half + 2 : 3 * half + 1]
    far_v = refs[3 * half + 1 : 4 * half + 1]
    outs = refs[4 * half + 1 + extra :]
    scale = own_q.shape[-1] ** (-0.5)
    k_all = jnp.concatenate(
        [own_k[...]] + [ref[1] for ref in near] + [ref[...] for ref in far], axis=0
    )
    v_all = jnp.concatenate(
        [own_v[...]] + [ref[...] for ref in near_v] + [ref[...] for ref in far_v], axis=0
    )
    tokens = own_q.shape[0]
    blocks = [own_q[...]] + [ref[0] for ref in near]
    for first in range(0, half, group):
        part = blocks[first : first + group]
        rows = jnp.concatenate(part, axis=0) if len(part) > 1 else part[0]
        scores = (
            lax.dot_general(
                rows, k_all, (((1,), (1,)), ((), ())), preferred_element_type=jnp.float32
            )
            * scale
        )
        top = jnp.max(scores, axis=1, keepdims=True)
        weights = jnp.exp(scores - top)
        total = jnp.sum(weights, axis=1, keepdims=True)
        mixed = (
            jnp.dot(weights.astype(jnp.bfloat16), v_all, preferred_element_type=jnp.float32)
            / total
        )
        mixed = mixed.astype(jnp.bfloat16)
        for i in range(len(part)):
            outs[first + i][...] = mixed[i * tokens : (i + 1) * tokens]


def attend(place, chunk, chunk_v, v_head, head, whole, after, width):
    own_q, own_k, near, far = chunk
    own_v, near_v, far_v = chunk_v
    tokens, wide = own_q.shape
    half = len(near) + 1
    keys = 2 * half * tokens
    group = max(1, min(half, (256 * 1024) // (keys * tokens)))
    heads = wide // HEAD_DIM
    class_heads = width // HEAD_DIM // half
    flat = pl.BlockSpec((tokens, HEAD_DIM), lambda h, *_: (0, h))
    value = pl.BlockSpec((tokens, HEAD_DIM), lambda h, *_: (0, v_head + h))
    stack = pl.BlockSpec((2, tokens, HEAD_DIM), lambda h, *_: (0, 0, h))
    column = pl.BlockSpec(
        (tokens, HEAD_DIM),
        lambda h, place_ref: (0, lax.rem(place_ref[0], half) * class_heads + head + h),
    )
    arrived = [in_hbm(array) for array in (*near, *far, *near_v, *far_v)]
    operands = [own_q, own_k, own_v, *arrived]
    specs = [flat, flat, value] + [stack] * (half - 1) + [flat] * half
    specs += [value] * (2 * half - 1)
    extras = list(after)
    aliases = {}
    if whole is not None:
        aliases = {1 + len(operands) + len(extras): 0}
        extras.append(whole)
    specs += [pl.BlockSpec(memory_space=pl.ANY)] * len(extras)
    return pl.pallas_call(
        functools.partial(attend_kernel, half, group, len(extras)),
        grid_spec=pltpu.PrefetchScalarGridSpec(
            num_scalar_prefetch=1,
            grid=(heads,),
            in_specs=specs,
            out_specs=[column] + [flat] * (half - 1),
        ),
        out_shape=[jax.ShapeDtypeStruct((tokens, width), jnp.bfloat16)]
        + [jax.ShapeDtypeStruct((tokens, wide), jnp.bfloat16)] * (half - 1),
        input_output_aliases=aliases,
        cost_estimate=pl.CostEstimate(
            flops=4 * heads * half * tokens * keys * HEAD_DIM,
            transcendentals=heads * half * tokens * keys,
            bytes_accessed=2 * heads * HEAD_DIM * (2 * half * tokens + 2 * keys),
        ),
        name="attend",
    )(place, *operands, *extras)


def join_kernel(half, class_wide, firsts, place_ref, *refs):
    count = len(firsts) * (half - 1)
    pieces, out, sems = refs[:count], refs[count + 1], refs[count + 2]
    place = lax.rem(place_ref[0], half)
    copies = []
    for i, first in enumerate(firsts):
        for mask in range(1, half):
            index = i * (half - 1) + mask - 1
            piece = pieces[index]
            start = pl.multiple_of((place ^ mask) * class_wide + first, HEAD_DIM)
            copies.append(
                pltpu.make_async_copy(
                    piece, out.at[:, pl.ds(start, piece.shape[1])], sems.at[index]
                )
            )
    for copy in copies:
        copy.start()
    for copy in copies:
        copy.wait()


def join(place, pieces, firsts, whole, half):
    if not pieces:
        return whole
    anywhere = pl.BlockSpec(memory_space=pl.ANY)
    return pl.pallas_call(
        functools.partial(join_kernel, half, whole.shape[1] // half, firsts),
        in_specs=[pl.BlockSpec(memory_space=pltpu.SMEM)] + [anywhere] * (len(pieces) + 1),
        out_specs=anywhere,
        out_shape=jax.ShapeDtypeStruct(whole.shape, whole.dtype),
        scratch_shapes=[pltpu.SemaphoreType.DMA((len(pieces),))],
        input_output_aliases={len(pieces) + 1: 0},
        name="join",
    )(place, *(in_hbm(piece) for piece in pieces), whole)


def conv_kernel(own_ref, one_ref, two_ref, weight_ref, latent_ref, bias_ref, out_ref, acc_ref):
    step = pl.program_id(0)
    rows, cols, chans = latent_ref.shape

    def add(frame_ref):
        for e in range(3):
            total = None
            for b in range(3):
                cells = frame_ref[b : b + rows].reshape(rows * cols, chans)
                part = jnp.dot(cells, weight_ref[0, b, e], preferred_element_type=jnp.float32)
                total = part if total is None else total + part

            @pl.when(step == 0)
            def _():
                acc_ref[e] = total

            @pl.when(step > 0)
            def _():
                acc_ref[e] += total

    @pl.when(step == 0)
    def _():
        add(two_ref)

    @pl.when(step == 1)
    def _():
        add(one_ref)

    @pl.when(step == 2)
    def _():
        add(own_ref)
        line = jnp.zeros((1, chans), jnp.float32)
        for row in range(rows):
            cells = pl.ds(row * cols, cols)
            left = jnp.concatenate([line, acc_ref[0, cells][: cols - 1]], axis=0)
            right = jnp.concatenate([acc_ref[2, cells][1:], line], axis=0)
            conv = left + acc_ref[1, cells] + right
            out_ref[row] = (
                latent_ref[row].astype(jnp.float32) + conv + bias_ref[...]
            ).astype(jnp.bfloat16)


def convolve(own, one_back, two_back, weight, latent, bias):
    rows, cols, chans = latent.shape
    frame = pl.BlockSpec(own.shape, lambda a: (0, 0, 0))
    image = pl.BlockSpec(latent.shape, lambda a: (0, 0, 0))
    return pl.pallas_call(
        conv_kernel,
        grid=(3,),
        in_specs=[
            frame,
            frame,
            frame,
            pl.BlockSpec((1,) + weight.shape[1:], lambda a: (a, 0, 0, 0, 0)),
            image,
            pl.BlockSpec(bias.shape, lambda a: (0,)),
        ],
        out_specs=image,
        out_shape=jax.ShapeDtypeStruct(latent.shape, jnp.bfloat16),
        scratch_shapes=[pltpu.VMEM((3, rows * cols, chans), jnp.float32)],
        cost_estimate=pl.CostEstimate(
            flops=2 * 27 * rows * cols * chans * chans,
            transcendentals=0,
            bytes_accessed=2 * 27 * chans * chans,
        ),
        name="convolve",
    )(own, one_back, two_back, weight, latent, bias)


def activate_kernel(place_ref, latent_ref, cache_ref, gain_ref, after_ref, *outs):
    own_ref, past_ref, last_ref, first_ref = outs

    def act(rows):
        rows = rows.astype(jnp.float32)
        mean_sq = jnp.mean(rows * rows, axis=-1, keepdims=True)
        return jax.nn.silu(rows * lax.rsqrt(mean_sq + EPSILON) * gain_ref[...]).astype(
            jnp.bfloat16
        )

    own = act(latent_ref[...])
    past = act(cache_ref[0])
    own_ref[...] = own
    past_ref[...] = past
    last_ref[0] = own[-1]
    last_ref[1] = past[-1]
    first_ref[0] = own[0]
    first_ref[1] = past[0]


def activate(place, latent, cache, gain, after):
    shape = latent.shape
    whole = pl.BlockSpec(shape, lambda i, *_: (0, 0, 0))
    edge_shape = (2,) + shape[1:]
    edge = pl.BlockSpec(edge_shape, lambda i, *_: (0, 0, 0))
    chosen = pl.BlockSpec(
        (1,) + shape, lambda i, place_ref: (jnp.minimum(place_ref[0], 1), 0, 0, 0)
    )
    gain_spec = pl.BlockSpec(gain.shape, lambda i, *_: (0,))
    return pl.pallas_call(
        activate_kernel,
        grid_spec=pltpu.PrefetchScalarGridSpec(
            num_scalar_prefetch=1,
            grid=(1,),
            in_specs=[whole, chosen, gain_spec, pl.BlockSpec(memory_space=pl.ANY)],
            out_specs=[whole, whole, edge, edge],
        ),
        out_shape=[jax.ShapeDtypeStruct(shape, jnp.bfloat16)] * 2
        + [jax.ShapeDtypeStruct(edge_shape, jnp.bfloat16)] * 2,
        name="activate",
    )(place, latent, cache, gain, after)


def decode(latent_frames, frame_cache, vae_gain, conv_weight, conv_bias, after):
    place = lax.axis_index("role").astype(jnp.int32)
    latent = latent_frames[0]
    own, past, last, first = activate(
        place[None], latent, frame_cache, vae_gain, after
    )
    below = shift(last, "seq", 1)
    above = shift(first, "seq", -1)
    extended = jnp.concatenate([below[:1], own, above[:1]], axis=0)
    past = jnp.concatenate([below[1:], past, above[1:]], axis=0)
    outgoing = jnp.where(place == lax.axis_size("role") - 1, past, extended)
    one_back = around(outgoing, "role", 1)
    two_back = around(outgoing, "role", 2)
    two_back = jnp.where(place == 0, past, two_back)
    decoded = convolve(extended, one_back, two_back, conv_weight, latent, conv_bias)
    return decoded, own


def body(
    queries,
    keys,
    values,
    q_gain,
    k_gain,
    latent_frames,
    frame_cache,
    vae_gain,
    conv_weight,
    conv_bias,
):
    width = queries.shape[2]
    half = lax.axis_size("seq") // 2
    chunks = chunks_of(width // HEAD_DIM // half)
    early = min(2, len(chunks))
    sizes = [heads * HEAD_DIM for heads in chunks]
    parts = [part for part in (sum(sizes[:early]), sum(sizes[early:])) if part]
    place = lax.axis_index("seq").astype(jnp.int32)[None]

    def send_values(own):
        near = [swap(own[mask], "seq", mask) for mask in range(1, half)]
        far = [swap(own[mask], "seq", half + mask) for mask in range(half)]
        return own[0], near, far

    own_v = split(place, values[0], half, parts)
    sent_v = [send_values(part) for part in own_v]
    decoded, activated = decode(
        latent_frames, frame_cache, vae_gain, conv_weight, conv_bias, own_v[0][0]
    )
    packed = pack(place, queries[0], keys[0], q_gain, k_gain, activated, half, sizes)
    ready = []
    for own_q, own_k, near, far in packed:
        near_in = [swap(near[mask - 1], "seq", mask) for mask in range(1, half)]
        far_in = [swap(own_k, "seq", half)]
        far_in += [swap(far[mask - 1], "seq", half + mask) for mask in range(1, half)]
        ready.append((own_q, own_k, near_in, far_in))
    whole, head, pieces, firsts = None, 0, [], []
    for index, chunk in enumerate(ready):
        part = 0 if index < early else 1
        v_head = head - (sum(chunks[:early]) if part else 0)
        after = [decoded] if index == early else []
        if index and index == len(ready) - 1:
            whole = join(place, pieces, firsts, whole, half)
            pieces, firsts = [], []
        whole, *mixed = attend(
            place, chunk, sent_v[part], v_head, head, whole, after, width
        )
        pieces += [swap(mixed[mask - 1], "seq", mask) for mask in range(1, half)]
        firsts.append(head * HEAD_DIM)
        head += chunks[index]
    attended = join(place, pieces, firsts, whole, half)[None]
    return (attended, decoded[None])


def solution(mesh):
    tokens = P(("groups", "role"), "seq", None)
    frames = P(("groups", "role"), "seq", None, None)
    return jax.shard_map(
        body,
        mesh=mesh,
        in_specs=(
            tokens,
            tokens,
            tokens,
            P(),
            P(),
            frames,
            P("groups", "seq", None, None),
            P(),
            P(),
            P(),
        ),
        out_specs=(tokens, frames),
        check_vma=False,
    )
```

```python
import functools

import jax
import jax.numpy as jnp
from jax import lax
from jax.experimental import pallas as pl
from jax.experimental.pallas import tpu as pltpu
from jax.sharding import PartitionSpec as P


HEAD_DIM = 128
EPSILON = 1e-06


def swap(value, axis, mask):
    count = lax.axis_size(axis)
    return lax.ppermute(value, axis, [(i, i ^ mask) for i in range(count)])


def shift(value, axis, steps):
    count = lax.axis_size(axis)
    return lax.ppermute(
        value, axis, [(i, i + steps) for i in range(count) if 0 <= i + steps < count]
    )


def around(value, axis, steps):
    count = lax.axis_size(axis)
    return lax.ppermute(value, axis, [(i, (i + steps) % count) for i in range(count)])


def in_hbm(array):
    return pltpu.with_memory_space_constraint(array, pltpu.HBM)


def chunks_of(heads):
    if heads % 8:
        return [heads]
    return [heads // 4] * 3 + [heads // 8] * 2


def split_kernel(half, parts, place_ref, v_ref, *refs):
    outs, sems = refs[:-1], refs[-1]
    place = lax.rem(place_ref[0], half)
    class_wide = sum(parts)
    copies = []
    first = 0
    for part, wide in enumerate(parts):
        for mask in range(half):
            start = pl.multiple_of((place ^ mask) * class_wide + first, HEAD_DIM)
            index = part * half + mask
            copies.append(
                pltpu.make_async_copy(
                    v_ref.at[:, pl.ds(start, wide)], outs[index], sems.at[index]
                )
            )
        first += wide
    for copy in copies:
        copy.start()
    for copy in copies:
        copy.wait()


def split(place, values, half, parts):
    tokens = values.shape[0]
    anywhere = pl.BlockSpec(memory_space=pl.ANY)
    outs = pl.pallas_call(
        functools.partial(split_kernel, half, parts),
        in_specs=[
            pl.BlockSpec(memory_space=pltpu.SMEM),
            pl.BlockSpec(memory_space=pltpu.VMEM),
        ],
        out_specs=[anywhere] * (half * len(parts)),
        out_shape=[
            jax.ShapeDtypeStruct((tokens, wide), values.dtype)
            for wide in parts
            for _ in range(half)
        ],
        scratch_shapes=[pltpu.SemaphoreType.DMA((half * len(parts),))],
        name="split",
    )(place, values)
    return [outs[i * half : (i + 1) * half] for i in range(len(parts))]


def pack_kernel(half, sizes, place_ref, q_ref, k_ref, qg_ref, kg_ref, after_ref, *outs):
    place = lax.rem(place_ref[0], half)

    def scale_of(ref):
        rows = ref[...].astype(jnp.float32)
        return lax.rsqrt(jnp.mean(rows * rows, axis=-1, keepdims=True) + EPSILON)

    q_scale = scale_of(q_ref)
    k_scale = scale_of(k_ref)
    class_wide = sum(sizes)
    outs = list(outs)
    first = 0
    for wide in sizes:
        for mask in range(half):
            start = pl.multiple_of((place ^ mask) * class_wide + first, HEAD_DIM)
            cols = pl.ds(start, wide)
            q_part = q_ref[:, cols].astype(jnp.float32) * q_scale * qg_ref[:, cols]
            k_part = k_ref[:, cols].astype(jnp.float32) * k_scale * kg_ref[:, cols]
            q_part = q_part.astype(jnp.bfloat16)
            k_part = k_part.astype(jnp.bfloat16)
            if mask == 0:
                outs.pop(0)[...] = q_part
                outs.pop(0)[...] = k_part
            else:
                near = outs.pop(0)
                near[0] = q_part
                near[1] = k_part
                outs.pop(0)[...] = k_part
        first += wide


def pack(place, queries, keys, q_gain, k_gain, after, half, sizes):
    tokens, width = queries.shape
    rows = min(tokens, 32)
    shapes, specs = [], []

    def add(wide, *lead):
        shapes.append(jax.ShapeDtypeStruct(lead + (tokens, wide), jnp.bfloat16))
        specs.append(
            pl.BlockSpec(lead + (rows, wide), lambda i, *_: (0,) * len(lead) + (i, 0))
        )

    for wide in sizes:
        add(wide)
        add(wide)
        for _ in range(1, half):
            add(wide, 2)
            add(wide)
    token_spec = pl.BlockSpec((rows, width), lambda i, *_: (i, 0))
    gain_spec = pl.BlockSpec((1, width), lambda i, *_: (0, 0))
    outs = pl.pallas_call(
        functools.partial(pack_kernel, half, sizes),
        grid_spec=pltpu.PrefetchScalarGridSpec(
            num_scalar_prefetch=1,
            grid=(tokens // rows,),
            in_specs=[token_spec] * 2
            + [gain_spec] * 2
            + [pl.BlockSpec(memory_space=pl.ANY)],
            out_specs=specs,
        ),
        out_shape=shapes,
        name="pack",
    )(place, queries, keys, q_gain[None], k_gain[None], after)
    outs = list(outs)
    result = []
    for _ in sizes:
        own_q, own_k = outs.pop(0), outs.pop(0)
        near, far = [], []
        for _ in range(1, half):
            near.append(outs.pop(0))
            far.append(outs.pop(0))
        result.append((own_q, own_k, near, far))
    return result


def attend_kernel(half, group, extra, place_ref, *refs):
    own_q, own_k, own_v = refs[:3]
    near = refs[3 : half + 2]
    far = refs[half + 2 : 2 * half + 2]
    near_v = refs[2 * half + 2 : 3 * half + 1]
    far_v = refs[3 * half + 1 : 4 * half + 1]
    outs = refs[4 * half + 1 + extra :]
    scale = own_q.shape[-1] ** (-0.5)
    k_all = jnp.concatenate(
        [own_k[...]] + [ref[1] for ref in near] + [ref[...] for ref in far], axis=0
    )
    v_all = jnp.concatenate(
        [own_v[...]] + [ref[...] for ref in near_v] + [ref[...] for ref in far_v], axis=0
    )
    tokens = own_q.shape[0]
    blocks = [own_q[...]] + [ref[0] for ref in near]
    for first in range(0, half, group):
        part = blocks[first : first + group]
        rows = jnp.concatenate(part, axis=0) if len(part) > 1 else part[0]
        scores = (
            lax.dot_general(
                rows, k_all, (((1,), (1,)), ((), ())), preferred_element_type=jnp.float32
            )
            * scale
        )
        top = jnp.max(scores, axis=1, keepdims=True)
        weights = jnp.exp(scores - top)
        total = jnp.sum(weights, axis=1, keepdims=True)
        mixed = (
            jnp.dot(weights.astype(jnp.bfloat16), v_all, preferred_element_type=jnp.float32)
            / total
        )
        mixed = mixed.astype(jnp.bfloat16)
        for i in range(len(part)):
            outs[first + i][...] = mixed[i * tokens : (i + 1) * tokens]


def attend(place, chunk, chunk_v, v_head, head, whole, after, width):
    own_q, own_k, near, far = chunk
    own_v, near_v, far_v = chunk_v
    tokens, wide = own_q.shape
    half = len(near) + 1
    keys = 2 * half * tokens
    group = max(1, min(half, (256 * 1024) // (keys * tokens)))
    heads = wide // HEAD_DIM
    class_heads = width // HEAD_DIM // half
    flat = pl.BlockSpec((tokens, HEAD_DIM), lambda h, *_: (0, h))
    value = pl.BlockSpec((tokens, HEAD_DIM), lambda h, *_: (0, v_head + h))
    stack = pl.BlockSpec((2, tokens, HEAD_DIM), lambda h, *_: (0, 0, h))
    column = pl.BlockSpec(
        (tokens, HEAD_DIM),
        lambda h, place_ref: (0, lax.rem(place_ref[0], half) * class_heads + head + h),
    )
    arrived = [in_hbm(array) for array in (*near, *far, *near_v, *far_v)]
    operands = [own_q, own_k, own_v, *arrived]
    specs = [flat, flat, value] + [stack] * (half - 1) + [flat] * half
    specs += [value] * (2 * half - 1)
    extras = list(after)
    aliases = {}
    if whole is not None:
        aliases = {1 + len(operands) + len(extras): 0}
        extras.append(whole)
    specs += [pl.BlockSpec(memory_space=pl.ANY)] * len(extras)
    return pl.pallas_call(
        functools.partial(attend_kernel, half, group, len(extras)),
        grid_spec=pltpu.PrefetchScalarGridSpec(
            num_scalar_prefetch=1,
            grid=(heads,),
            in_specs=specs,
            out_specs=[column] + [flat] * (half - 1),
        ),
        out_shape=[jax.ShapeDtypeStruct((tokens, width), jnp.bfloat16)]
        + [jax.ShapeDtypeStruct((tokens, wide), jnp.bfloat16)] * (half - 1),
        input_output_aliases=aliases,
        cost_estimate=pl.CostEstimate(
            flops=4 * heads * half * tokens * keys * HEAD_DIM,
            transcendentals=heads * half * tokens * keys,
            bytes_accessed=2 * heads * HEAD_DIM * (2 * half * tokens + 2 * keys),
        ),
        name="attend",
    )(place, *operands, *extras)


def join_kernel(half, class_wide, firsts, place_ref, *refs):
    count = len(firsts) * (half - 1)
    pieces, out, sems = refs[:count], refs[count + 1], refs[count + 2]
    place = lax.rem(place_ref[0], half)
    copies = []
    for i, first in enumerate(firsts):
        for mask in range(1, half):
            index = i * (half - 1) + mask - 1
            piece = pieces[index]
            start = pl.multiple_of((place ^ mask) * class_wide + first, HEAD_DIM)
            copies.append(
                pltpu.make_async_copy(
                    piece, out.at[:, pl.ds(start, piece.shape[1])], sems.at[index]
                )
            )
    for copy in copies:
        copy.start()
    for copy in copies:
        copy.wait()


def join(place, pieces, firsts, whole, half):
    if not pieces:
        return whole
    anywhere = pl.BlockSpec(memory_space=pl.ANY)
    return pl.pallas_call(
        functools.partial(join_kernel, half, whole.shape[1] // half, firsts),
        in_specs=[pl.BlockSpec(memory_space=pltpu.SMEM)]
        + [pl.BlockSpec(memory_space=pltpu.VMEM)] * len(pieces)
        + [anywhere],
        out_specs=anywhere,
        out_shape=jax.ShapeDtypeStruct(whole.shape, whole.dtype),
        scratch_shapes=[pltpu.SemaphoreType.DMA((len(pieces),))],
        input_output_aliases={len(pieces) + 1: 0},
        name="join",
    )(place, *(in_hbm(piece) for piece in pieces), whole)


def conv_kernel(own_ref, one_ref, two_ref, weight_ref, latent_ref, bias_ref, out_ref, acc_ref):
    step = pl.program_id(0)
    rows, cols, chans = latent_ref.shape

    def add(frame_ref):
        for e in range(3):
            total = None
            for b in range(3):
                cells = frame_ref[b : b + rows].reshape(rows * cols, chans)
                part = jnp.dot(cells, weight_ref[0, b, e], preferred_element_type=jnp.float32)
                total = part if total is None else total + part

            @pl.when(step == 0)
            def _():
                acc_ref[e] = total

            @pl.when(step > 0)
            def _():
                acc_ref[e] += total

    @pl.when(step == 0)
    def _():
        add(two_ref)

    @pl.when(step == 1)
    def _():
        add(one_ref)

    @pl.when(step == 2)
    def _():
        add(own_ref)
        line = jnp.zeros((1, chans), jnp.float32)
        for row in range(rows):
            cells = pl.ds(row * cols, cols)
            left = jnp.concatenate([line, acc_ref[0, cells][: cols - 1]], axis=0)
            right = jnp.concatenate([acc_ref[2, cells][1:], line], axis=0)
            conv = left + acc_ref[1, cells] + right
            out_ref[row] = (
                latent_ref[row].astype(jnp.float32) + conv + bias_ref[...]
            ).astype(jnp.bfloat16)


def convolve(own, one_back, two_back, weight, latent, bias):
    rows, cols, chans = latent.shape
    frame = pl.BlockSpec(own.shape, lambda a: (0, 0, 0))
    image = pl.BlockSpec(latent.shape, lambda a: (0, 0, 0))
    return pl.pallas_call(
        conv_kernel,
        grid=(3,),
        in_specs=[
            frame,
            frame,
            frame,
            pl.BlockSpec((1,) + weight.shape[1:], lambda a: (a, 0, 0, 0, 0)),
            image,
            pl.BlockSpec(bias.shape, lambda a: (0,)),
        ],
        out_specs=image,
        out_shape=jax.ShapeDtypeStruct(latent.shape, jnp.bfloat16),
        scratch_shapes=[pltpu.VMEM((3, rows * cols, chans), jnp.float32)],
        cost_estimate=pl.CostEstimate(
            flops=2 * 27 * rows * cols * chans * chans,
            transcendentals=0,
            bytes_accessed=2 * 27 * chans * chans,
        ),
        name="convolve",
    )(own, one_back, two_back, weight, latent, bias)


def activate_kernel(place_ref, latent_ref, cache_ref, gain_ref, after_ref, *outs):
    own_ref, past_ref, last_ref, first_ref = outs

    def act(rows):
        rows = rows.astype(jnp.float32)
        mean_sq = jnp.mean(rows * rows, axis=-1, keepdims=True)
        return jax.nn.silu(rows * lax.rsqrt(mean_sq + EPSILON) * gain_ref[...]).astype(
            jnp.bfloat16
        )

    own = act(latent_ref[...])
    past = act(cache_ref[0])
    own_ref[...] = own
    past_ref[...] = past
    last_ref[0] = own[-1]
    last_ref[1] = past[-1]
    first_ref[0] = own[0]
    first_ref[1] = past[0]


def activate(place, latent, cache, gain, after):
    shape = latent.shape
    whole = pl.BlockSpec(shape, lambda i, *_: (0, 0, 0))
    edge_shape = (2,) + shape[1:]
    edge = pl.BlockSpec(edge_shape, lambda i, *_: (0, 0, 0))
    chosen = pl.BlockSpec(
        (1,) + shape, lambda i, place_ref: (jnp.minimum(place_ref[0], 1), 0, 0, 0)
    )
    gain_spec = pl.BlockSpec(gain.shape, lambda i, *_: (0,))
    return pl.pallas_call(
        activate_kernel,
        grid_spec=pltpu.PrefetchScalarGridSpec(
            num_scalar_prefetch=1,
            grid=(1,),
            in_specs=[whole, chosen, gain_spec, pl.BlockSpec(memory_space=pl.ANY)],
            out_specs=[whole, whole, edge, edge],
        ),
        out_shape=[jax.ShapeDtypeStruct(shape, jnp.bfloat16)] * 2
        + [jax.ShapeDtypeStruct(edge_shape, jnp.bfloat16)] * 2,
        name="activate",
    )(place, latent, cache, gain, after)


def decode(latent_frames, frame_cache, vae_gain, conv_weight, conv_bias, after):
    place = lax.axis_index("role").astype(jnp.int32)
    latent = latent_frames[0]
    own, past, last, first = activate(
        place[None], latent, frame_cache, vae_gain, after
    )
    below = shift(last, "seq", 1)
    above = shift(first, "seq", -1)
    extended = jnp.concatenate([below[:1], own, above[:1]], axis=0)
    past = jnp.concatenate([below[1:], past, above[1:]], axis=0)
    outgoing = jnp.where(place == lax.axis_size("role") - 1, past, extended)
    one_back = around(outgoing, "role", 1)
    two_back = around(outgoing, "role", 2)
    two_back = jnp.where(place == 0, past, two_back)
    decoded = convolve(extended, one_back, two_back, conv_weight, latent, conv_bias)
    return decoded, own


def body(
    queries,
    keys,
    values,
    q_gain,
    k_gain,
    latent_frames,
    frame_cache,
    vae_gain,
    conv_weight,
    conv_bias,
):
    width = queries.shape[2]
    half = lax.axis_size("seq") // 2
    chunks = chunks_of(width // HEAD_DIM // half)
    early = min(2, len(chunks))
    sizes = [heads * HEAD_DIM for heads in chunks]
    parts = [part for part in (sum(sizes[:early]), sum(sizes[early:])) if part]
    place = lax.axis_index("seq").astype(jnp.int32)[None]

    def send_values(own):
        near = [swap(own[mask], "seq", mask) for mask in range(1, half)]
        far = [swap(own[mask], "seq", half + mask) for mask in range(half)]
        return own[0], near, far

    own_v = split(place, values[0], half, parts)
    sent_v = [send_values(part) for part in own_v]
    decoded, activated = decode(
        latent_frames, frame_cache, vae_gain, conv_weight, conv_bias, own_v[0][0]
    )
    packed = pack(place, queries[0], keys[0], q_gain, k_gain, activated, half, sizes)
    ready = []
    for own_q, own_k, near, far in packed:
        near_in = [swap(near[mask - 1], "seq", mask) for mask in range(1, half)]
        far_in = [swap(own_k, "seq", half)]
        far_in += [swap(far[mask - 1], "seq", half + mask) for mask in range(1, half)]
        ready.append((own_q, own_k, near_in, far_in))
    whole, head, pieces, firsts = None, 0, [], []
    for index, chunk in enumerate(ready):
        part = 0 if index < early else 1
        v_head = head - (sum(chunks[:early]) if part else 0)
        after = [decoded] if index == early else []
        whole, *mixed = attend(
            place, chunk, sent_v[part], v_head, head, whole, after, width
        )
        pieces += [swap(mixed[mask - 1], "seq", mask) for mask in range(1, half)]
        firsts.append(head * HEAD_DIM)
        head += chunks[index]
    late = half - 1
    whole = join(place, pieces[: len(pieces) - late], firsts[:-1], whole, half)
    attended = join(place, pieces[len(pieces) - late :], firsts[-1:], whole, half)[None]
    return (attended, decoded[None])


def solution(mesh):
    tokens = P(("groups", "role"), "seq", None)
    frames = P(("groups", "role"), "seq", None, None)
    return jax.shard_map(
        body,
        mesh=mesh,
        in_specs=(
            tokens,
            tokens,
            tokens,
            P(),
            P(),
            frames,
            P("groups", "seq", None, None),
            P(),
            P(),
            P(),
        ),
        out_specs=(tokens, frames),
        check_vma=False,
    )
```

```python
import functools

import jax
import jax.numpy as jnp
from jax import lax
from jax.experimental import pallas as pl
from jax.experimental.pallas import tpu as pltpu
from jax.sharding import PartitionSpec as P


HEAD_DIM = 128
EPSILON = 1e-06
RESIDENT = True
SHARES = (4, 4, 4, 2, 2)
EARLY = 2


def swap(value, axis, mask):
    count = lax.axis_size(axis)
    return lax.ppermute(value, axis, [(i, i ^ mask) for i in range(count)])


def to_neighbour(value, steps, ends):
    rows, roles = lax.axis_size("seq"), lax.axis_size("role")
    pairs = [
        (row * roles + role, (row + steps) * roles + role)
        for row in range(rows)
        for role in range(roles)
        if 0 <= row + steps < rows and (not ends or role in (0, roles - 1))
    ]
    return lax.ppermute(value, ("seq", "role"), pairs)


def around(value, axis, steps):
    count = lax.axis_size(axis)
    return lax.ppermute(value, axis, [(i, (i + steps) % count) for i in range(count)])


def in_vmem(array):
    return pltpu.with_memory_space_constraint(array, pltpu.VMEM)


def chunks_of(heads):
    total = sum(SHARES)
    return [heads] if heads % total else [share * heads // total for share in SHARES]


def split_kernel(half, class_wide, place_ref, v_ref, *refs):
    outs, (held, sems) = refs[:half], refs[half:]
    place = lax.rem(place_ref[0], half)
    wide = held.shape[2]
    loads, stores = [], []
    for mask in range(half):
        start = pl.multiple_of((place ^ mask) * class_wide, HEAD_DIM)
        columns = v_ref.at[:, pl.ds(start, wide)]
        loads.append(pltpu.make_async_copy(columns, held.at[mask], sems.at[0, mask]))
        stores.append(pltpu.make_async_copy(held.at[mask], outs[mask], sems.at[1, mask]))
    for load in loads:
        load.start()
    for load, store in zip(loads, stores):
        load.wait()
        store.start()
    for store in stores:
        store.wait()


def split(place, values, half, wide):
    tokens, width = values.shape
    anywhere = pl.BlockSpec(memory_space=pl.ANY)
    return pl.pallas_call(
        functools.partial(split_kernel, half, width // half),
        in_specs=[pl.BlockSpec(memory_space=pltpu.SMEM), anywhere],
        out_specs=[anywhere] * half,
        out_shape=[jax.ShapeDtypeStruct((tokens, wide), values.dtype)] * half,
        scratch_shapes=[
            pltpu.VMEM((half, tokens, wide), values.dtype),
            pltpu.SemaphoreType.DMA((2, half)),
        ],
        name="split",
    )(place, values)


def pack_kernel(half, sizes, early, place_ref, q_ref, k_ref, v_ref, qg_ref, kg_ref, *outs):
    place = lax.rem(place_ref[0], half)

    def scale_of(ref):
        rows = ref[...].astype(jnp.float32)
        return lax.rsqrt(jnp.mean(rows * rows, axis=-1, keepdims=True) + EPSILON)

    q_scale = scale_of(q_ref)
    k_scale = scale_of(k_ref)
    class_wide = sum(sizes)
    outs = list(outs[1:])
    first = 0
    for index, wide in enumerate(sizes):
        for mask in range(half):
            start = pl.multiple_of((place ^ mask) * class_wide + first, HEAD_DIM)
            cols = pl.ds(start, wide)
            q_part = q_ref[:, cols].astype(jnp.float32) * q_scale * qg_ref[:, cols]
            k_part = k_ref[:, cols].astype(jnp.float32) * k_scale * kg_ref[:, cols]
            parts = [q_part.astype(jnp.bfloat16), k_part.astype(jnp.bfloat16)]
            if index >= early:
                parts.append(v_ref[:, cols])
            near, far = outs.pop(0), outs.pop(0)
            for i, part in enumerate(parts):
                if mask:
                    near[i] = part
                elif i == 0:
                    near[...] = part
                if i:
                    far[i - 1] = part
        first += wide


def pack(place, queries, keys, values, q_gain, k_gain, after, half, sizes, early):
    tokens, width = queries.shape
    rows = min(tokens, 32)
    shapes, specs = [], []

    def add(wide, *lead):
        shapes.append(jax.ShapeDtypeStruct(lead + (tokens, wide), jnp.bfloat16))
        specs.append(
            pl.BlockSpec(lead + (rows, wide), lambda i, *_: (0,) * len(lead) + (i, 0))
        )

    for index, wide in enumerate(sizes):
        count = 3 if index >= early else 2
        for mask in range(half):
            if mask:
                add(wide, count)
            else:
                add(wide)
            add(wide, count - 1)
    token_spec = pl.BlockSpec((rows, width), lambda i, *_: (i, 0))
    gain_spec = pl.BlockSpec((1, width), lambda i, *_: (0, 0))
    outs = pl.pallas_call(
        functools.partial(pack_kernel, half, sizes, early),
        grid_spec=pltpu.PrefetchScalarGridSpec(
            num_scalar_prefetch=1,
            grid=(tokens // rows,),
            in_specs=[token_spec] * 3
            + [gain_spec] * 2
            + [pl.BlockSpec(memory_space=pl.ANY)],
            out_specs=specs,
        ),
        out_shape=shapes,
        name="pack",
    )(place, queries, keys, values, q_gain[None], k_gain[None], after)
    return [
        (outs[2 * i * half : 2 * (i + 1) * half : 2], outs[2 * i * half + 1 : 2 * (i + 1) * half : 2])
        for i in range(len(sizes))
    ]


def mix(rows, k_all, v_all, scale):
    scores = (
        lax.dot_general(
            rows, k_all, (((1,), (1,)), ((), ())), preferred_element_type=jnp.float32
        )
        * scale
    )
    top = jnp.max(scores, axis=1, keepdims=True)
    weights = jnp.exp(scores - top)
    total = jnp.sum(weights, axis=1, keepdims=True)
    mixed = jnp.dot(weights.astype(jnp.bfloat16), v_all, preferred_element_type=jnp.float32)
    return (mixed / total).astype(jnp.bfloat16)


def head_of(parts, group, read, scale):
    blocks, keys, values = ([read(*entry) for entry in entries] for entries in parts)
    k_all = jnp.concatenate(keys, axis=0)
    v_all = jnp.concatenate(values, axis=0)
    tokens = blocks[0].shape[0]
    outs = []
    for first in range(0, len(blocks), group):
        part = blocks[first : first + group]
        rows = jnp.concatenate(part, axis=0) if len(part) > 1 else part[0]
        mixed = mix(rows, k_all, v_all, scale)
        outs += [mixed[i * tokens : (i + 1) * tokens] for i in range(len(part))]
    return outs


def attend_kernel(parts, group, count, extra, place_ref, *refs):
    def read(operand, index):
        return refs[operand][...] if index is None else refs[operand][index]

    outs = refs[count + extra :]
    for out, piece in zip(outs, head_of(parts, group, read, HEAD_DIM ** (-0.5))):
        out[...] = piece


def attend_resident_kernel(parts, group, count, extra, offsets, half, head, place_ref, *refs):
    whole, *sends, mine, sems = refs[count + extra :]
    first_column = lax.rem(place_ref[0], half) * (whole.shape[1] // half) + head * HEAD_DIM
    copies = []
    for h in range(mine.shape[1] // HEAD_DIM):

        def read(operand, index):
            start = (offsets[operand] + h) * HEAD_DIM
            cols = slice(start, start + HEAD_DIM)
            ref = refs[operand]
            return ref[:, cols] if index is None else ref[index, :, cols]

        cols = slice(h * HEAD_DIM, (h + 1) * HEAD_DIM)
        pieces = head_of(parts, group, read, HEAD_DIM ** (-0.5))
        for out, piece in zip([mine, *sends], pieces):
            out[:, cols] = piece
        column = pl.multiple_of(first_column + h * HEAD_DIM, HEAD_DIM)
        copies.append(
            pltpu.make_async_copy(
                mine.at[:, cols], whole.at[:, pl.ds(column, HEAD_DIM)], sems.at[h]
            )
        )
        copies[-1].start()
    for copy in copies:
        copy.wait()


def attend(place, chunk, v_chunk, v_head, head, whole, width, resident):
    own_q, own_kv, near, far = chunk
    tokens, wide = own_q.shape
    half = len(near) + 1
    keys = 2 * half * tokens
    group = max(1, min(half, (256 * 1024) // (keys * tokens)))
    heads = wide // HEAD_DIM
    class_heads = width // HEAD_DIM // half
    operands = [own_q, own_kv, *near, *far]
    nears = range(2, half + 1)
    fars = range(half + 1, 2 * half + 1)
    q_parts = [(0, None)] + [(i, 0) for i in nears]
    k_parts = [(1, 0)] + [(i, 1) for i in nears] + [(i, 0) for i in fars]
    offsets = [0] * len(operands)
    if v_chunk is None:
        v_parts = [(1, 1)] + [(i, 2) for i in nears] + [(i, 1) for i in fars]
    else:
        v_parts = [(len(operands) + i, None) for i in range(len(v_chunk))]
        operands += v_chunk
        offsets += [v_head] * len(v_chunk)
    parts = (q_parts, k_parts, v_parts)
    anywhere = pl.BlockSpec(memory_space=pl.ANY)
    extras, aliases = [], {}
    if whole is not None:
        aliases = {1 + len(operands): 0}
        extras = [whole]
    shapes = [jax.ShapeDtypeStruct((tokens, width), jnp.bfloat16)]
    shapes += [jax.ShapeDtypeStruct((tokens, wide), jnp.bfloat16)] * (half - 1)
    common = dict(
        out_shape=shapes,
        input_output_aliases=aliases,
        cost_estimate=pl.CostEstimate(
            flops=4 * heads * half * tokens * keys * HEAD_DIM,
            transcendentals=heads * half * tokens * keys,
            bytes_accessed=2 * heads * HEAD_DIM * (2 * half * tokens + 2 * keys),
        ),
        name="attend",
    )
    if resident:
        vmem = pl.BlockSpec(memory_space=pltpu.VMEM)
        return pl.pallas_call(
            functools.partial(
                attend_resident_kernel,
                parts,
                group,
                len(operands),
                len(extras),
                offsets,
                half,
                head,
            ),
            in_specs=[pl.BlockSpec(memory_space=pltpu.SMEM)]
            + [vmem] * len(operands)
            + [anywhere] * len(extras),
            out_specs=[anywhere] + [vmem] * (half - 1),
            scratch_shapes=[
                pltpu.VMEM((tokens, wide), jnp.bfloat16),
                pltpu.SemaphoreType.DMA((heads,)),
            ],
            **common,
        )(place, *(in_vmem(array) for array in operands), *extras)

    def spec(array, offset):
        lead = array.shape[:-2]
        return pl.BlockSpec(
            lead + (tokens, HEAD_DIM), lambda h, *_: (0,) * len(lead) + (0, offset + h)
        )

    column = pl.BlockSpec(
        (tokens, HEAD_DIM),
        lambda h, place_ref: (0, lax.rem(place_ref[0], half) * class_heads + head + h),
    )
    flat = pl.BlockSpec((tokens, HEAD_DIM), lambda h, *_: (0, h))
    return pl.pallas_call(
        functools.partial(attend_kernel, parts, group, len(operands), len(extras)),
        grid_spec=pltpu.PrefetchScalarGridSpec(
            num_scalar_prefetch=1,
            grid=(heads,),
            in_specs=[spec(array, offset) for array, offset in zip(operands, offsets)]
            + [anywhere] * len(extras),
            out_specs=[column] + [flat] * (half - 1),
        ),
        **common,
    )(place, *operands, *extras)


def join_kernel(half, class_wide, firsts, place_ref, *refs):
    count = len(firsts) * (half - 1)
    pieces, out, sems = refs[:count], refs[count + 1], refs[count + 2]
    place = lax.rem(place_ref[0], half)
    copies = []
    for i, first in enumerate(firsts):
        for mask in range(1, half):
            index = i * (half - 1) + mask - 1
            piece = pieces[index]
            start = pl.multiple_of((place ^ mask) * class_wide + first, HEAD_DIM)
            copies.append(
                pltpu.make_async_copy(
                    piece, out.at[:, pl.ds(start, piece.shape[1])], sems.at[index]
                )
            )
    for copy in copies:
        copy.start()
    for copy in copies:
        copy.wait()


def join(place, pieces, firsts, whole, half):
    if not pieces:
        return whole
    anywhere = pl.BlockSpec(memory_space=pl.ANY)
    return pl.pallas_call(
        functools.partial(join_kernel, half, whole.shape[1] // half, firsts),
        in_specs=[pl.BlockSpec(memory_space=pltpu.SMEM)]
        + [pl.BlockSpec(memory_space=pltpu.VMEM)] * len(pieces)
        + [anywhere],
        out_specs=anywhere,
        out_shape=jax.ShapeDtypeStruct(whole.shape, whole.dtype),
        scratch_shapes=[pltpu.SemaphoreType.DMA((len(pieces),))],
        input_output_aliases={len(pieces) + 1: 0},
        name="join",
    )(place, *(in_vmem(piece) for piece in pieces), whole)


def conv_kernel(own_ref, one_ref, two_ref, weight_ref, latent_ref, bias_ref, out_ref, acc_ref):
    step = pl.program_id(0)
    rows, cols, chans = latent_ref.shape

    def add(frame_ref):
        for e in range(3):
            total = None
            for b in range(3):
                cells = frame_ref[b : b + rows].reshape(rows * cols, chans)
                part = jnp.dot(cells, weight_ref[0, b, e], preferred_element_type=jnp.float32)
                total = part if total is None else total + part

            @pl.when(step == 0)
            def _():
                acc_ref[e] = total

            @pl.when(step > 0)
            def _():
                acc_ref[e] += total

    @pl.when(step == 0)
    def _():
        add(two_ref)

    @pl.when(step == 1)
    def _():
        add(one_ref)

    @pl.when(step == 2)
    def _():
        add(own_ref)
        line = jnp.zeros((1, chans), jnp.float32)
        for row in range(rows):
            cells = pl.ds(row * cols, cols)
            left = jnp.concatenate([line, acc_ref[0, cells][: cols - 1]], axis=0)
            right = jnp.concatenate([acc_ref[2, cells][1:], line], axis=0)
            conv = left + acc_ref[1, cells] + right
            out_ref[row] = (
                latent_ref[row].astype(jnp.float32) + conv + bias_ref[...]
            ).astype(jnp.bfloat16)


def convolve(own, one_back, two_back, weight, latent, bias):
    rows, cols, chans = latent.shape
    frame = pl.BlockSpec(own.shape, lambda a: (0, 0, 0))
    image = pl.BlockSpec(latent.shape, lambda a: (0, 0, 0))
    return pl.pallas_call(
        conv_kernel,
        grid=(3,),
        in_specs=[
            frame,
            frame,
            frame,
            pl.BlockSpec((1,) + weight.shape[1:], lambda a: (a, 0, 0, 0, 0)),
            image,
            pl.BlockSpec(bias.shape, lambda a: (0,)),
        ],
        out_specs=image,
        out_shape=jax.ShapeDtypeStruct(latent.shape, jnp.bfloat16),
        scratch_shapes=[pltpu.VMEM((3, rows * cols, chans), jnp.float32)],
        cost_estimate=pl.CostEstimate(
            flops=2 * 27 * rows * cols * chans * chans,
            transcendentals=0,
            bytes_accessed=2 * 27 * chans * chans,
        ),
        name="convolve",
    )(own, one_back, two_back, weight, latent, bias)


def activate_kernel(place_ref, latent_ref, cache_ref, gain_ref, after_ref, *outs):
    own_ref, past_ref, own_last, own_first, past_last, past_first = outs

    def act(rows):
        rows = rows.astype(jnp.float32)
        mean_sq = jnp.mean(rows * rows, axis=-1, keepdims=True)
        return jax.nn.silu(rows * lax.rsqrt(mean_sq + EPSILON) * gain_ref[...]).astype(
            jnp.bfloat16
        )

    own = act(latent_ref[...])
    past = act(cache_ref[0])
    own_ref[...] = own
    past_ref[...] = past
    own_last[0] = own[-1]
    own_first[0] = own[0]
    past_last[0] = past[-1]
    past_first[0] = past[0]


def activate(place, latent, cache, gain, after):
    shape = latent.shape
    whole = pl.BlockSpec(shape, lambda i, *_: (0, 0, 0))
    edge_shape = (1,) + shape[1:]
    edge = pl.BlockSpec(edge_shape, lambda i, *_: (0, 0, 0))
    chosen = pl.BlockSpec(
        (1,) + shape, lambda i, place_ref: (jnp.minimum(place_ref[0], 1), 0, 0, 0)
    )
    gain_spec = pl.BlockSpec(gain.shape, lambda i, *_: (0,))
    return pl.pallas_call(
        activate_kernel,
        grid_spec=pltpu.PrefetchScalarGridSpec(
            num_scalar_prefetch=1,
            grid=(1,),
            in_specs=[whole, chosen, gain_spec, pl.BlockSpec(memory_space=pl.ANY)],
            out_specs=[whole] * 2 + [edge] * 4,
        ),
        out_shape=[jax.ShapeDtypeStruct(shape, jnp.bfloat16)] * 2
        + [jax.ShapeDtypeStruct(edge_shape, jnp.bfloat16)] * 4,
        name="activate",
    )(place, latent, cache, gain, after)


def decode(latent_frames, frame_cache, vae_gain, conv_weight, conv_bias, after):
    place = lax.axis_index("role").astype(jnp.int32)
    latent = latent_frames[0]
    own, past, *edges = activate(place[None], latent, frame_cache, vae_gain, after)
    halos = []
    for i, edge in enumerate(edges):
        halos.append(to_neighbour(edge, 1 if i % 2 == 0 else -1, i >= 2))
    extended = jnp.concatenate([halos[0], own, halos[1]], axis=0)
    past = jnp.concatenate([halos[2], past, halos[3]], axis=0)
    outgoing = jnp.where(place == lax.axis_size("role") - 1, past, extended)
    one_back = around(outgoing, "role", 1)
    two_back = around(outgoing, "role", 2)
    two_back = jnp.where(place == 0, past, two_back)
    decoded = convolve(extended, one_back, two_back, conv_weight, latent, conv_bias)
    return decoded, own


def body(
    queries,
    keys,
    values,
    q_gain,
    k_gain,
    latent_frames,
    frame_cache,
    vae_gain,
    conv_weight,
    conv_bias,
):
    width = queries.shape[2]
    half = lax.axis_size("seq") // 2
    chunks = chunks_of(width // HEAD_DIM // half)
    early = min(EARLY, len(chunks))
    sizes = [heads * HEAD_DIM for heads in chunks]
    place = lax.axis_index("seq").astype(jnp.int32)[None]

    def exchange(near, far):
        arrived = [swap(near[mask], "seq", mask) for mask in range(1, half)]
        return arrived, [swap(far[mask], "seq", half + mask) for mask in range(half)]

    first_v = split(place, values[0], half, sum(sizes[:early]))
    near, far = exchange(first_v, first_v)
    v_chunk = [first_v[0], *near, *far]
    decoded, activated = decode(
        latent_frames, frame_cache, vae_gain, conv_weight, conv_bias, first_v[0]
    )
    packed = pack(
        place, queries[0], keys[0], values[0], q_gain, k_gain, activated, half, sizes, early
    )
    ready = []
    for near, far in packed:
        ready.append((near[0], far[0], *exchange(near, far)))
    whole, head, pieces, firsts = None, 0, [], []
    for index, chunk in enumerate(ready):
        whole, *mixed = attend(
            place,
            chunk,
            v_chunk if index < early else None,
            head,
            head,
            whole,
            width,
            RESIDENT and chunks[index] < chunks[0],
        )
        pieces += [swap(mixed[mask - 1], "seq", mask) for mask in range(1, half)]
        firsts.append(head * HEAD_DIM)
        head += chunks[index]
    late = half - 1
    whole = join(place, pieces[: len(pieces) - late], firsts[:-1], whole, half)
    attended = join(place, pieces[len(pieces) - late :], firsts[-1:], whole, half)[None]
    return (attended, decoded[None])


def solution(mesh):
    tokens = P(("groups", "role"), "seq", None)
    frames = P(("groups", "role"), "seq", None, None)
    return jax.shard_map(
        body,
        mesh=mesh,
        in_specs=(
            tokens,
            tokens,
            tokens,
            P(),
            P(),
            frames,
            P("groups", "seq", None, None),
            P(),
            P(),
            P(),
        ),
        out_specs=(tokens, frames),
        check_vma=False,
    )
```

```python
import functools

import jax
import jax.numpy as jnp
from jax import lax
from jax.experimental import pallas as pl
from jax.experimental.pallas import tpu as pltpu
from jax.sharding import PartitionSpec as P


HEAD_DIM = 128
EPSILON = 1e-06
RESIDENT = True
SHARED = 2
SHARES = (4, 4, 2, 2)
EARLY = 2
FEW = 8


def swap(value, axis, mask):
    count = lax.axis_size(axis)
    return lax.ppermute(value, axis, [(i, i ^ mask) for i in range(count)])


def to_neighbour(value, steps, ends):
    rows, roles = lax.axis_size("seq"), lax.axis_size("role")
    pairs = [
        (row * roles + role, (row + steps) * roles + role)
        for row in range(rows)
        for role in range(roles)
        if 0 <= row + steps < rows and (not ends or role in (0, roles - 1))
    ]
    return lax.ppermute(value, ("seq", "role"), pairs)


def around(value, axis, steps):
    count = lax.axis_size(axis)
    return lax.ppermute(value, axis, [(i, (i + steps) % count) for i in range(count)])


def in_vmem(array):
    return pltpu.with_memory_space_constraint(array, pltpu.VMEM)


def chunks_of(heads, ring):
    half = ring // 2
    rest, odd = divmod(heads - SHARED * ring, half)
    total = sum(SHARES)
    if odd or rest <= 0 or rest % total:
        return [(half, heads // half, 0, heads // half)]
    chunks = [(ring, SHARED, 0, SHARED)] if SHARED else []
    base = SHARED * ring
    for share in SHARES:
        chunks.append((half, rest * share // total, base, rest))
        base += rest * share // total
    return chunks


def first_column(place, mask, chunk):
    span, _, base, stride = chunk
    return pl.multiple_of((base + ((place ^ mask) % span) * stride) * HEAD_DIM, HEAD_DIM)


def split_kernel(ring, chunks, place_ref, v_ref, *refs):
    outs, sems = refs[:ring], refs[ring]
    copies = []
    for mask in range(ring):
        at = 0
        for i, chunk in enumerate(chunks):
            wide = chunk[1] * HEAD_DIM
            columns = v_ref.at[:, pl.ds(first_column(place_ref[0], mask, chunk), wide)]
            target = outs[mask].at[:, pl.ds(at, wide)]
            copies.append(pltpu.make_async_copy(columns, target, sems.at[i, mask]))
            at += wide
    for copy in copies:
        copy.start()
    for copy in copies:
        copy.wait()


def split(place, values, ring, chunks):
    tokens = values.shape[0]
    wide = sum(chunk[1] for chunk in chunks) * HEAD_DIM
    kind = pltpu.VMEM if ring <= FEW else jax.ShapeDtypeStruct
    return pl.pallas_call(
        functools.partial(split_kernel, ring, chunks),
        in_specs=[
            pl.BlockSpec(memory_space=pltpu.SMEM),
            pl.BlockSpec(memory_space=pl.ANY),
        ],
        out_specs=[pl.BlockSpec(memory_space=pltpu.VMEM)] * ring,
        out_shape=[kind((tokens, wide), values.dtype)] * ring,
        scratch_shapes=[pltpu.SemaphoreType.DMA((len(chunks), ring))],
        name="split",
    )(place, values)


def pack_kernel(ring, chunks, early, place_ref, q_ref, k_ref, v_ref, qg_ref, kg_ref, *outs):
    place = place_ref[0]

    def scale_of(ref):
        rows = ref[...].astype(jnp.float32)
        return lax.rsqrt(jnp.mean(rows * rows, axis=-1, keepdims=True) + EPSILON)

    q_scale = scale_of(q_ref)
    k_scale = scale_of(k_ref)
    outs = list(outs)
    for index, chunk in enumerate(chunks):
        for mask in range(chunk[0]):
            cols = pl.ds(first_column(place, mask, chunk), chunk[1] * HEAD_DIM)
            q_part = q_ref[:, cols].astype(jnp.float32) * q_scale * qg_ref[:, cols]
            k_part = k_ref[:, cols].astype(jnp.float32) * k_scale * kg_ref[:, cols]
            parts = [q_part.astype(jnp.bfloat16), k_part.astype(jnp.bfloat16)]
            if index >= early:
                parts.append(v_ref[:, cols])
            near = outs.pop(0)
            if mask:
                for i, part in enumerate(parts):
                    near[i] = part
            else:
                near[...] = parts[0]
            if mask == 0 or chunk[0] < ring:
                far = outs.pop(0)
                for i, part in enumerate(parts[1:]):
                    far[i] = part


def pack(place, queries, keys, values, q_gain, k_gain, ring, chunks, early):
    tokens, width = queries.shape
    rows = min(tokens, 32)
    shapes, specs = [], []

    def add(wide, *lead):
        shapes.append(jax.ShapeDtypeStruct(lead + (tokens, wide), jnp.bfloat16))
        specs.append(
            pl.BlockSpec(lead + (rows, wide), lambda i, *_: (0,) * len(lead) + (i, 0))
        )

    for index, (span, heads, _, _) in enumerate(chunks):
        count = 3 if index >= early else 2
        for mask in range(span):
            if mask:
                add(heads * HEAD_DIM, count)
            else:
                add(heads * HEAD_DIM)
            if mask == 0 or span < ring:
                add(heads * HEAD_DIM, count - 1)
    token_spec = pl.BlockSpec((rows, width), lambda i, *_: (i, 0))
    gain_spec = pl.BlockSpec((1, width), lambda i, *_: (0, 0))
    outs = pl.pallas_call(
        functools.partial(pack_kernel, ring, chunks, early),
        grid_spec=pltpu.PrefetchScalarGridSpec(
            num_scalar_prefetch=1,
            grid=(tokens // rows,),
            in_specs=[token_spec] * 3 + [gain_spec] * 2,
            out_specs=specs,
        ),
        out_shape=shapes,
        name="pack",
    )(place, queries, keys, values, q_gain[None], k_gain[None])
    outs = list(outs)
    result = []
    for span, *_ in chunks:
        near, far = [], []
        for mask in range(span):
            near.append(outs.pop(0))
            if mask == 0 or span < ring:
                far.append(outs.pop(0))
        result.append((near, far))
    return result


def mix(rows, k_all, v_all, scale):
    scores = (
        lax.dot_general(
            rows, k_all, (((1,), (1,)), ((), ())), preferred_element_type=jnp.float32
        )
        * scale
    )
    top = jnp.max(scores, axis=1, keepdims=True)
    weights = jnp.exp(scores - top)
    total = jnp.sum(weights, axis=1, keepdims=True)
    mixed = jnp.dot(weights.astype(jnp.bfloat16), v_all, preferred_element_type=jnp.float32)
    return (mixed / total).astype(jnp.bfloat16)


def head_of(parts, group, read, scale):
    blocks, keys, values = ([read(*entry) for entry in entries] for entries in parts)
    k_all = jnp.concatenate(keys, axis=0)
    v_all = jnp.concatenate(values, axis=0)
    tokens = blocks[0].shape[0]
    outs = []
    for first in range(0, len(blocks), group):
        part = blocks[first : first + group]
        rows = jnp.concatenate(part, axis=0) if len(part) > 1 else part[0]
        mixed = mix(rows, k_all, v_all, scale)
        outs += [mixed[i * tokens : (i + 1) * tokens] for i in range(len(part))]
    return outs


def attend_kernel(parts, group, count, extra, place_ref, *refs):
    def read(operand, index):
        return refs[operand][...] if index is None else refs[operand][index]

    outs = refs[count + extra :]
    for out, piece in zip(outs, head_of(parts, group, read, HEAD_DIM ** (-0.5))):
        out[...] = piece


def attend_resident_kernel(parts, group, count, extra, offsets, chunk, place_ref, *refs):
    whole, *sends, mine, sems = refs[count + extra :]
    start_column = first_column(place_ref[0], 0, chunk)
    copies = []
    for h in range(chunk[1]):

        def read(operand, index):
            start = (offsets[operand] + h) * HEAD_DIM
            cols = slice(start, start + HEAD_DIM)
            ref = refs[operand]
            return ref[:, cols] if index is None else ref[index, :, cols]

        cols = slice(h * HEAD_DIM, (h + 1) * HEAD_DIM)
        pieces = head_of(parts, group, read, HEAD_DIM ** (-0.5))
        for out, piece in zip([mine, *sends], pieces):
            out[:, cols] = piece
        column = pl.multiple_of(start_column + h * HEAD_DIM, HEAD_DIM)
        copies.append(
            pltpu.make_async_copy(
                mine.at[:, cols], whole.at[:, pl.ds(column, HEAD_DIM)], sems.at[h]
            )
        )
        copies[-1].start()
    for copy in copies:
        copy.wait()


def attend(place, chunk, arrays, v_arrays, v_head, whole, width, resident):
    own_q, own_kv, near, far = arrays
    span, heads, base, stride = chunk
    tokens, wide = own_q.shape
    keys = (1 + len(near) + len(far)) * tokens
    group = max(1, min(span, (128 * 1024) // (keys * tokens)))
    operands = [own_q, own_kv, *near, *far]
    nears = range(2, span + 1)
    fars = range(span + 1, span + 1 + len(far))
    q_parts = [(0, None)] + [(i, 0) for i in nears]
    k_parts = [(1, 0)] + [(i, 1) for i in nears] + [(i, 0) for i in fars]
    offsets = [0] * len(operands)
    if v_arrays is None:
        v_parts = [(1, 1)] + [(i, 2) for i in nears] + [(i, 1) for i in fars]
    else:
        v_parts = [(len(operands) + i, None) for i in range(len(v_arrays))]
        operands += v_arrays
        offsets += [v_head] * len(v_arrays)
    parts = (q_parts, k_parts, v_parts)
    anywhere = pl.BlockSpec(memory_space=pl.ANY)
    extras, aliases = [], {}
    if whole is not None:
        aliases = {1 + len(operands): 0}
        extras = [whole]
    kind = pltpu.VMEM if resident else jax.ShapeDtypeStruct
    shapes = [jax.ShapeDtypeStruct((tokens, width), jnp.bfloat16)]
    shapes += [kind((tokens, wide), jnp.bfloat16)] * (span - 1)
    common = dict(
        out_shape=shapes,
        input_output_aliases=aliases,
        cost_estimate=pl.CostEstimate(
            flops=4 * heads * span * tokens * keys * HEAD_DIM,
            transcendentals=heads * span * tokens * keys,
            bytes_accessed=2 * heads * HEAD_DIM * (2 * span * tokens + 2 * keys),
        ),
        name="attend",
    )
    if resident:
        vmem = pl.BlockSpec(memory_space=pltpu.VMEM)
        return pl.pallas_call(
            functools.partial(
                attend_resident_kernel,
                parts,
                group,
                len(operands),
                len(extras),
                offsets,
                chunk,
            ),
            in_specs=[pl.BlockSpec(memory_space=pltpu.SMEM)]
            + [vmem] * len(operands)
            + [anywhere] * len(extras),
            out_specs=[anywhere] + [vmem] * (span - 1),
            scratch_shapes=[
                pltpu.VMEM((tokens, wide), jnp.bfloat16),
                pltpu.SemaphoreType.DMA((heads,)),
            ],
            **common,
        )(place, *(in_vmem(array) for array in operands), *extras)

    def spec(array, offset):
        lead = array.shape[:-2]
        return pl.BlockSpec(
            lead + (tokens, HEAD_DIM), lambda h, *_: (0,) * len(lead) + (0, offset + h)
        )

    column = pl.BlockSpec(
        (tokens, HEAD_DIM),
        lambda h, place_ref: (0, base + lax.rem(place_ref[0], span) * stride + h),
    )
    flat = pl.BlockSpec((tokens, HEAD_DIM), lambda h, *_: (0, h))
    return pl.pallas_call(
        functools.partial(attend_kernel, parts, group, len(operands), len(extras)),
        grid_spec=pltpu.PrefetchScalarGridSpec(
            num_scalar_prefetch=1,
            grid=(heads,),
            in_specs=[spec(array, offset) for array, offset in zip(operands, offsets)]
            + [anywhere] * len(extras),
            out_specs=[column] + [flat] * (span - 1),
        ),
        **common,
    )(place, *operands, *extras)


def join_kernel(where, place_ref, *refs):
    pieces, out, sems = refs[: len(where)], refs[-2], refs[-1]
    copies = []
    for i, (mask, chunk) in enumerate(where):
        columns = pl.ds(first_column(place_ref[0], mask, chunk), pieces[i].shape[1])
        copies.append(pltpu.make_async_copy(pieces[i], out.at[:, columns], sems.at[i]))
    for copy in copies:
        copy.start()
    for copy in copies:
        copy.wait()


def join(place, pieces, where, whole):
    if not pieces:
        return whole
    anywhere = pl.BlockSpec(memory_space=pl.ANY)
    return pl.pallas_call(
        functools.partial(join_kernel, where),
        in_specs=[pl.BlockSpec(memory_space=pltpu.SMEM)]
        + [pl.BlockSpec(memory_space=pltpu.VMEM)] * len(pieces)
        + [anywhere],
        out_specs=anywhere,
        out_shape=jax.ShapeDtypeStruct(whole.shape, whole.dtype),
        scratch_shapes=[pltpu.SemaphoreType.DMA((len(pieces),))],
        input_output_aliases={len(pieces) + 1: 0},
        name="join",
    )(place, *(in_vmem(piece) for piece in pieces), whole)


def conv_kernel(own_ref, one_ref, two_ref, weight_ref, latent_ref, bias_ref, out_ref, acc_ref):
    step = pl.program_id(0)
    rows, cols, chans = latent_ref.shape

    def add(frame_ref):
        for e in range(3):
            total = None
            for b in range(3):
                cells = frame_ref[b : b + rows].reshape(rows * cols, chans)
                part = jnp.dot(cells, weight_ref[0, b, e], preferred_element_type=jnp.float32)
                total = part if total is None else total + part

            @pl.when(step == 0)
            def _():
                acc_ref[e] = total

            @pl.when(step > 0)
            def _():
                acc_ref[e] += total

    @pl.when(step == 0)
    def _():
        add(two_ref)

    @pl.when(step == 1)
    def _():
        add(one_ref)

    @pl.when(step == 2)
    def _():
        add(own_ref)
        line = jnp.zeros((1, chans), jnp.float32)
        for row in range(rows):
            cells = pl.ds(row * cols, cols)
            left = jnp.concatenate([line, acc_ref[0, cells][: cols - 1]], axis=0)
            right = jnp.concatenate([acc_ref[2, cells][1:], line], axis=0)
            conv = left + acc_ref[1, cells] + right
            out_ref[row] = (
                latent_ref[row].astype(jnp.float32) + conv + bias_ref[...]
            ).astype(jnp.bfloat16)


def convolve(own, one_back, two_back, weight, latent, bias):
    rows, cols, chans = latent.shape
    frame = pl.BlockSpec(own.shape, lambda a: (0, 0, 0))
    image = pl.BlockSpec(latent.shape, lambda a: (0, 0, 0))
    return pl.pallas_call(
        conv_kernel,
        grid=(3,),
        in_specs=[
            frame,
            frame,
            frame,
            pl.BlockSpec((1,) + weight.shape[1:], lambda a: (a, 0, 0, 0, 0)),
            image,
            pl.BlockSpec(bias.shape, lambda a: (0,)),
        ],
        out_specs=image,
        out_shape=jax.ShapeDtypeStruct(latent.shape, jnp.bfloat16),
        scratch_shapes=[pltpu.VMEM((3, rows * cols, chans), jnp.float32)],
        cost_estimate=pl.CostEstimate(
            flops=2 * 27 * rows * cols * chans * chans,
            transcendentals=0,
            bytes_accessed=2 * 27 * chans * chans,
        ),
        name="convolve",
    )(own, one_back, two_back, weight, latent, bias)


def activate_kernel(place_ref, latent_ref, cache_ref, gain_ref, *outs):
    own_ref, past_ref, own_last, own_first, past_last, past_first = outs

    def act(rows):
        rows = rows.astype(jnp.float32)
        mean_sq = jnp.mean(rows * rows, axis=-1, keepdims=True)
        return jax.nn.silu(rows * lax.rsqrt(mean_sq + EPSILON) * gain_ref[...]).astype(
            jnp.bfloat16
        )

    own = act(latent_ref[...])
    past = act(cache_ref[0])
    own_ref[...] = own
    past_ref[...] = past
    own_last[0] = own[-1]
    own_first[0] = own[0]
    past_last[0] = past[-1]
    past_first[0] = past[0]


def activate(place, latent, cache, gain):
    shape = latent.shape
    whole = pl.BlockSpec(shape, lambda i, *_: (0, 0, 0))
    edge_shape = (1,) + shape[1:]
    edge = pl.BlockSpec(edge_shape, lambda i, *_: (0, 0, 0))
    chosen = pl.BlockSpec(
        (1,) + shape, lambda i, place_ref: (jnp.minimum(place_ref[0], 1), 0, 0, 0)
    )
    gain_spec = pl.BlockSpec(gain.shape, lambda i, *_: (0,))
    return pl.pallas_call(
        activate_kernel,
        grid_spec=pltpu.PrefetchScalarGridSpec(
            num_scalar_prefetch=1,
            grid=(1,),
            in_specs=[whole, chosen, gain_spec],
            out_specs=[whole] * 2 + [edge] * 4,
        ),
        out_shape=[jax.ShapeDtypeStruct(shape, jnp.bfloat16)] * 2
        + [jax.ShapeDtypeStruct(edge_shape, jnp.bfloat16)] * 4,
        name="activate",
    )(place, latent, cache, gain)


def decode(latent_frames, frame_cache, vae_gain, conv_weight, conv_bias):
    place = lax.axis_index("role").astype(jnp.int32)
    latent = latent_frames[0]
    own, past, *edges = activate(place[None], latent, frame_cache, vae_gain)
    halos = []
    for i, edge in enumerate(edges):
        halos.append(to_neighbour(edge, 1 if i % 2 == 0 else -1, i >= 2))
    extended = jnp.concatenate([halos[0], own, halos[1]], axis=0)
    past = jnp.concatenate([halos[2], past, halos[3]], axis=0)
    outgoing = jnp.where(place == lax.axis_size("role") - 1, past, extended)
    one_back = around(outgoing, "role", 1)
    two_back = around(outgoing, "role", 2)
    two_back = jnp.where(place == 0, past, two_back)
    decoded = convolve(extended, one_back, two_back, conv_weight, latent, conv_bias)
    return decoded


def body(
    queries,
    keys,
    values,
    q_gain,
    k_gain,
    latent_frames,
    frame_cache,
    vae_gain,
    conv_weight,
    conv_bias,
):
    width = queries.shape[2]
    ring = lax.axis_size("seq")
    chunks = chunks_of(width // HEAD_DIM, ring)
    early = min(EARLY, len(chunks))
    place = lax.axis_index("seq").astype(jnp.int32)[None]

    first_v = split(place, values[0], ring, chunks[:early])
    v_arrays = [first_v[0]]
    v_arrays += [swap(first_v[mask], "seq", mask) for mask in range(1, ring)]
    decoded = decode(latent_frames, frame_cache, vae_gain, conv_weight, conv_bias)
    packed = pack(
        place, queries[0], keys[0], values[0], q_gain, k_gain, ring, chunks, early
    )
    ready = []
    for index, (near, far) in enumerate(packed):
        span = chunks[index][0]
        near_in = [swap(near[mask], "seq", mask) for mask in range(1, span)]
        far_in = [swap(far[mask % span], "seq", mask) for mask in range(span, ring)]
        ready.append((near[0], far[0], near_in, far_in))
    whole, v_head, pieces, where = None, 0, [], []
    for index, chunk in enumerate(chunks):
        whole, *mixed = attend(
            place,
            chunk,
            ready[index],
            v_arrays if index < early else None,
            v_head,
            whole,
            width,
            RESIDENT and index >= early and chunk[1] < chunks[early][1],
        )
        v_head += chunk[1]
        for mask in range(1, chunk[0]):
            pieces.append(swap(mixed[mask - 1], "seq", mask))
            where.append((mask, chunk))
    last = len(pieces) - chunks[-1][0] + 1
    whole = join(place, pieces[:last], where[:last], whole)
    attended = join(place, pieces[last:], where[last:], whole)[None]
    return (attended, decoded[None])


def solution(mesh):
    tokens = P(("groups", "role"), "seq", None)
    frames = P(("groups", "role"), "seq", None, None)
    return jax.shard_map(
        body,
        mesh=mesh,
        in_specs=(
            tokens,
            tokens,
            tokens,
            P(),
            P(),
            frames,
            P("groups", "seq", None, None),
            P(),
            P(),
            P(),
        ),
        out_specs=(tokens, frames),
        check_vma=False,
    )
```

```python
import functools

import jax
import jax.numpy as jnp
from jax import lax
from jax.experimental import pallas as pl
from jax.experimental.pallas import tpu as pltpu
from jax.sharding import PartitionSpec as P


HEAD_DIM = 128
EPSILON = 1e-06
RESIDENT = True
SHARED = 2
SHARES = (4, 4, 2, 2)
EARLY = 2
FEW = 8


def swap(value, axis, mask):
    count = lax.axis_size(axis)
    return lax.ppermute(value, axis, [(i, i ^ mask) for i in range(count)])


def to_neighbour(value, steps, ends):
    rows, roles = lax.axis_size("seq"), lax.axis_size("role")
    pairs = [
        (row * roles + role, (row + steps) * roles + role)
        for row in range(rows)
        for role in range(roles)
        if 0 <= row + steps < rows and (not ends or role in (0, roles - 1))
    ]
    return lax.ppermute(value, ("seq", "role"), pairs)


def around(value, axis, steps):
    count = lax.axis_size(axis)
    return lax.ppermute(value, axis, [(i, (i + steps) % count) for i in range(count)])


def in_vmem(array):
    return pltpu.with_memory_space_constraint(array, pltpu.VMEM)


def chunks_of(heads, ring):
    half = ring // 2
    rest, odd = divmod(heads - SHARED * ring, half)
    total = sum(SHARES)
    if odd or rest <= 0 or rest % total:
        return [(half, heads // half, 0, heads // half)]
    chunks = [(ring, SHARED, 0, SHARED)] if SHARED else []
    base = SHARED * ring
    for share in SHARES:
        chunks.append((half, rest * share // total, base, rest))
        base += rest * share // total
    return chunks


def first_column(place, mask, chunk):
    span, _, base, stride = chunk
    return pl.multiple_of((base + ((place ^ mask) % span) * stride) * HEAD_DIM, HEAD_DIM)


def split_kernel(ring, chunks, place_ref, v_ref, *refs):
    outs, sems = refs[:ring], refs[ring]
    copies = []
    for mask in range(ring):
        at = 0
        for i, chunk in enumerate(chunks):
            wide = chunk[1] * HEAD_DIM
            columns = v_ref.at[:, pl.ds(first_column(place_ref[0], mask, chunk), wide)]
            target = outs[mask].at[:, pl.ds(at, wide)]
            copies.append(pltpu.make_async_copy(columns, target, sems.at[i, mask]))
            at += wide
    for copy in copies:
        copy.start()
    for copy in copies:
        copy.wait()


def split(place, values, ring, chunks):
    tokens = values.shape[0]
    wide = sum(chunk[1] for chunk in chunks) * HEAD_DIM
    kind = pltpu.VMEM if ring <= FEW else jax.ShapeDtypeStruct
    return pl.pallas_call(
        functools.partial(split_kernel, ring, chunks),
        in_specs=[
            pl.BlockSpec(memory_space=pltpu.SMEM),
            pl.BlockSpec(memory_space=pl.ANY),
        ],
        out_specs=[pl.BlockSpec(memory_space=pltpu.VMEM)] * ring,
        out_shape=[kind((tokens, wide), values.dtype)] * ring,
        scratch_shapes=[pltpu.SemaphoreType.DMA((len(chunks), ring))],
        name="split",
    )(place, values)


def pack_kernel(ring, chunks, early, place_ref, q_ref, k_ref, v_ref, qg_ref, kg_ref, *outs):
    place = place_ref[0]

    def scale_of(ref):
        rows = ref[...].astype(jnp.float32)
        return lax.rsqrt(jnp.mean(rows * rows, axis=-1, keepdims=True) + EPSILON)

    q_scale = scale_of(q_ref)
    k_scale = scale_of(k_ref)
    outs = list(outs)
    for index, chunk in enumerate(chunks):
        for mask in range(chunk[0]):
            cols = pl.ds(first_column(place, mask, chunk), chunk[1] * HEAD_DIM)
            q_part = q_ref[:, cols].astype(jnp.float32) * q_scale * qg_ref[:, cols]
            k_part = k_ref[:, cols].astype(jnp.float32) * k_scale * kg_ref[:, cols]
            parts = [q_part.astype(jnp.bfloat16), k_part.astype(jnp.bfloat16)]
            if index >= early:
                parts.append(v_ref[:, cols])
            near = outs.pop(0)
            if mask:
                for i, part in enumerate(parts):
                    near[i] = part
            else:
                near[...] = parts[0]
            if mask == 0 or chunk[0] < ring:
                far = outs.pop(0)
                for i, part in enumerate(parts[1:]):
                    far[i] = part


def pack(place, queries, keys, values, q_gain, k_gain, ring, chunks, early):
    tokens, width = queries.shape
    rows = min(tokens, 32)
    shapes, specs = [], []

    def add(wide, *lead):
        shapes.append(jax.ShapeDtypeStruct(lead + (tokens, wide), jnp.bfloat16))
        specs.append(
            pl.BlockSpec(lead + (rows, wide), lambda i, *_: (0,) * len(lead) + (i, 0))
        )

    for index, (span, heads, _, _) in enumerate(chunks):
        count = 3 if index >= early else 2
        for mask in range(span):
            if mask:
                add(heads * HEAD_DIM, count)
            else:
                add(heads * HEAD_DIM)
            if mask == 0 or span < ring:
                add(heads * HEAD_DIM, count - 1)
    token_spec = pl.BlockSpec((rows, width), lambda i, *_: (i, 0))
    gain_spec = pl.BlockSpec((1, width), lambda i, *_: (0, 0))
    outs = pl.pallas_call(
        functools.partial(pack_kernel, ring, chunks, early),
        grid_spec=pltpu.PrefetchScalarGridSpec(
            num_scalar_prefetch=1,
            grid=(tokens // rows,),
            in_specs=[token_spec] * 3 + [gain_spec] * 2,
            out_specs=specs,
        ),
        out_shape=shapes,
        name="pack",
    )(place, queries, keys, values, q_gain[None], k_gain[None])
    outs = list(outs)
    result = []
    for span, *_ in chunks:
        near, far = [], []
        for mask in range(span):
            near.append(outs.pop(0))
            if mask == 0 or span < ring:
                far.append(outs.pop(0))
        result.append((near, far))
    return result


def mix(rows, k_all, v_all, scale):
    scores = (
        lax.dot_general(
            rows, k_all, (((1,), (1,)), ((), ())), preferred_element_type=jnp.float32
        )
        * scale
    )
    top = jnp.max(scores, axis=1, keepdims=True)
    weights = jnp.exp(scores - top)
    total = jnp.sum(weights, axis=1, keepdims=True)
    mixed = jnp.dot(weights.astype(jnp.bfloat16), v_all, preferred_element_type=jnp.float32)
    return (mixed / total).astype(jnp.bfloat16)


def head_of(parts, group, read, scale):
    blocks, keys, values = ([read(*entry) for entry in entries] for entries in parts)
    k_all = jnp.concatenate(keys, axis=0)
    v_all = jnp.concatenate(values, axis=0)
    tokens = blocks[0].shape[0]
    outs = []
    for first in range(0, len(blocks), group):
        part = blocks[first : first + group]
        rows = jnp.concatenate(part, axis=0) if len(part) > 1 else part[0]
        mixed = mix(rows, k_all, v_all, scale)
        outs += [mixed[i * tokens : (i + 1) * tokens] for i in range(len(part))]
    return outs


def attend_kernel(parts, group, count, extra, place_ref, *refs):
    def read(operand, index):
        return refs[operand][...] if index is None else refs[operand][index]

    outs = refs[count + extra :]
    for out, piece in zip(outs, head_of(parts, group, read, HEAD_DIM ** (-0.5))):
        out[...] = piece


def attend_resident_kernel(parts, group, count, extra, offsets, chunk, place_ref, *refs):
    whole, *sends, mine, sems = refs[count + extra :]
    start_column = first_column(place_ref[0], 0, chunk)
    copies = []
    for h in range(chunk[1]):

        def read(operand, index):
            start = (offsets[operand] + h) * HEAD_DIM
            cols = slice(start, start + HEAD_DIM)
            ref = refs[operand]
            return ref[:, cols] if index is None else ref[index, :, cols]

        cols = slice(h * HEAD_DIM, (h + 1) * HEAD_DIM)
        pieces = head_of(parts, group, read, HEAD_DIM ** (-0.5))
        for out, piece in zip([mine, *sends], pieces):
            out[:, cols] = piece
        column = pl.multiple_of(start_column + h * HEAD_DIM, HEAD_DIM)
        copies.append(
            pltpu.make_async_copy(
                mine.at[:, cols], whole.at[:, pl.ds(column, HEAD_DIM)], sems.at[h]
            )
        )
        copies[-1].start()
    for copy in copies:
        copy.wait()


def attend(place, chunk, arrays, v_arrays, v_head, whole, width, resident):
    own_q, own_kv, near, far = arrays
    span, heads, base, stride = chunk
    tokens, wide = own_q.shape
    keys = (1 + len(near) + len(far)) * tokens
    group = max(1, min(span, (128 * 1024) // (keys * tokens)))
    operands = [own_q, own_kv, *near, *far]
    nears = range(2, span + 1)
    fars = range(span + 1, span + 1 + len(far))
    q_parts = [(0, None)] + [(i, 0) for i in nears]
    k_parts = [(1, 0)] + [(i, 1) for i in nears] + [(i, 0) for i in fars]
    offsets = [0] * len(operands)
    if v_arrays is None:
        v_parts = [(1, 1)] + [(i, 2) for i in nears] + [(i, 1) for i in fars]
    else:
        v_parts = [(len(operands) + i, None) for i in range(len(v_arrays))]
        operands += v_arrays
        offsets += [v_head] * len(v_arrays)
    parts = (q_parts, k_parts, v_parts)
    anywhere = pl.BlockSpec(memory_space=pl.ANY)
    extras, aliases = [], {}
    if whole is not None:
        aliases = {1 + len(operands): 0}
        extras = [whole]
    kind = pltpu.VMEM if resident else jax.ShapeDtypeStruct
    shapes = [jax.ShapeDtypeStruct((tokens, width), jnp.bfloat16)]
    shapes += [kind((tokens, wide), jnp.bfloat16)] * (span - 1)
    common = dict(
        out_shape=shapes,
        input_output_aliases=aliases,
        cost_estimate=pl.CostEstimate(
            flops=4 * heads * span * tokens * keys * HEAD_DIM,
            transcendentals=heads * span * tokens * keys,
            bytes_accessed=2 * heads * HEAD_DIM * (2 * span * tokens + 2 * keys),
        ),
        name="attend",
    )
    if resident:
        vmem = pl.BlockSpec(memory_space=pltpu.VMEM)
        return pl.pallas_call(
            functools.partial(
                attend_resident_kernel,
                parts,
                group,
                len(operands),
                len(extras),
                offsets,
                chunk,
            ),
            in_specs=[pl.BlockSpec(memory_space=pltpu.SMEM)]
            + [vmem] * len(operands)
            + [anywhere] * len(extras),
            out_specs=[anywhere] + [vmem] * (span - 1),
            scratch_shapes=[
                pltpu.VMEM((tokens, wide), jnp.bfloat16),
                pltpu.SemaphoreType.DMA((heads,)),
            ],
            **common,
        )(place, *(in_vmem(array) for array in operands), *extras)

    def spec(array, offset):
        lead = array.shape[:-2]
        return pl.BlockSpec(
            lead + (tokens, HEAD_DIM), lambda h, *_: (0,) * len(lead) + (0, offset + h)
        )

    column = pl.BlockSpec(
        (tokens, HEAD_DIM),
        lambda h, place_ref: (0, base + lax.rem(place_ref[0], span) * stride + h),
    )
    flat = pl.BlockSpec((tokens, HEAD_DIM), lambda h, *_: (0, h))
    return pl.pallas_call(
        functools.partial(attend_kernel, parts, group, len(operands), len(extras)),
        grid_spec=pltpu.PrefetchScalarGridSpec(
            num_scalar_prefetch=1,
            grid=(heads,),
            in_specs=[spec(array, offset) for array, offset in zip(operands, offsets)]
            + [anywhere] * len(extras),
            out_specs=[column] + [flat] * (span - 1),
        ),
        **common,
    )(place, *operands, *extras)


def join_kernel(where, place_ref, *refs):
    pieces, out, sems = refs[: len(where)], refs[-2], refs[-1]
    copies = []
    for i, (mask, chunk) in enumerate(where):
        columns = pl.ds(first_column(place_ref[0], mask, chunk), pieces[i].shape[1])
        copies.append(pltpu.make_async_copy(pieces[i], out.at[:, columns], sems.at[i]))
    for copy in copies:
        copy.start()
    for copy in copies:
        copy.wait()


def join(place, pieces, where, whole):
    if not pieces:
        return whole
    anywhere = pl.BlockSpec(memory_space=pl.ANY)
    return pl.pallas_call(
        functools.partial(join_kernel, where),
        in_specs=[pl.BlockSpec(memory_space=pltpu.SMEM)]
        + [pl.BlockSpec(memory_space=pltpu.VMEM)] * len(pieces)
        + [anywhere],
        out_specs=anywhere,
        out_shape=jax.ShapeDtypeStruct(whole.shape, whole.dtype),
        scratch_shapes=[pltpu.SemaphoreType.DMA((len(pieces),))],
        input_output_aliases={len(pieces) + 1: 0},
        name="join",
    )(place, *(in_vmem(piece) for piece in pieces), whole)


def conv_kernel(own_ref, one_ref, two_ref, weight_ref, latent_ref, bias_ref, out_ref, acc_ref):
    step = pl.program_id(0)
    rows, cols, chans = latent_ref.shape

    def add(frame_ref):
        for e in range(3):
            total = None
            for b in range(3):
                cells = frame_ref[b : b + rows].reshape(rows * cols, chans)
                part = jnp.dot(cells, weight_ref[0, b, e], preferred_element_type=jnp.float32)
                total = part if total is None else total + part

            @pl.when(step == 0)
            def _():
                acc_ref[e] = total

            @pl.when(step > 0)
            def _():
                acc_ref[e] += total

    @pl.when(step == 0)
    def _():
        add(two_ref)

    @pl.when(step == 1)
    def _():
        add(one_ref)

    @pl.when(step == 2)
    def _():
        add(own_ref)
        line = jnp.zeros((1, chans), jnp.float32)
        for row in range(rows):
            cells = pl.ds(row * cols, cols)
            left = jnp.concatenate([line, acc_ref[0, cells][: cols - 1]], axis=0)
            right = jnp.concatenate([acc_ref[2, cells][1:], line], axis=0)
            conv = left + acc_ref[1, cells] + right
            out_ref[row] = (
                latent_ref[row].astype(jnp.float32) + conv + bias_ref[...]
            ).astype(jnp.bfloat16)


def convolve(own, one_back, two_back, weight, latent, bias):
    rows, cols, chans = latent.shape
    frame = pl.BlockSpec(own.shape, lambda a: (0, 0, 0))
    image = pl.BlockSpec(latent.shape, lambda a: (0, 0, 0))
    return pl.pallas_call(
        conv_kernel,
        grid=(3,),
        in_specs=[
            frame,
            frame,
            frame,
            pl.BlockSpec((1,) + weight.shape[1:], lambda a: (a, 0, 0, 0, 0)),
            image,
            pl.BlockSpec(bias.shape, lambda a: (0,)),
        ],
        out_specs=image,
        out_shape=jax.ShapeDtypeStruct(latent.shape, jnp.bfloat16),
        scratch_shapes=[pltpu.VMEM((3, rows * cols, chans), jnp.float32)],
        cost_estimate=pl.CostEstimate(
            flops=2 * 27 * rows * cols * chans * chans,
            transcendentals=0,
            bytes_accessed=2 * 27 * chans * chans,
        ),
        name="convolve",
    )(own, one_back, two_back, weight, latent, bias)


def activate_kernel(place_ref, latent_ref, cache_ref, gain_ref, *outs):
    own_ref, past_ref, own_last, own_first, past_last, past_first = outs

    def act(rows):
        rows = rows.astype(jnp.float32)
        mean_sq = jnp.mean(rows * rows, axis=-1, keepdims=True)
        return jax.nn.silu(rows * lax.rsqrt(mean_sq + EPSILON) * gain_ref[...]).astype(
            jnp.bfloat16
        )

    own = act(latent_ref[...])
    past = act(cache_ref[0])
    own_ref[...] = own
    past_ref[...] = past
    own_last[0] = own[-1]
    own_first[0] = own[0]
    past_last[0] = past[-1]
    past_first[0] = past[0]


def activate(place, latent, cache, gain):
    shape = latent.shape
    whole = pl.BlockSpec(shape, lambda i, *_: (0, 0, 0))
    edge_shape = (1,) + shape[1:]
    edge = pl.BlockSpec(edge_shape, lambda i, *_: (0, 0, 0))
    chosen = pl.BlockSpec(
        (1,) + shape, lambda i, place_ref: (jnp.minimum(place_ref[0], 1), 0, 0, 0)
    )
    gain_spec = pl.BlockSpec(gain.shape, lambda i, *_: (0,))
    return pl.pallas_call(
        activate_kernel,
        grid_spec=pltpu.PrefetchScalarGridSpec(
            num_scalar_prefetch=1,
            grid=(1,),
            in_specs=[whole, chosen, gain_spec],
            out_specs=[whole] * 2 + [edge] * 4,
        ),
        out_shape=[jax.ShapeDtypeStruct(shape, jnp.bfloat16)] * 2
        + [jax.ShapeDtypeStruct(edge_shape, jnp.bfloat16)] * 4,
        name="activate",
    )(place, latent, cache, gain)


def decode(latent_frames, frame_cache, vae_gain, conv_weight, conv_bias):
    place = lax.axis_index("role").astype(jnp.int32)
    latent = latent_frames[0]
    own, past, *edges = activate(place[None], latent, frame_cache, vae_gain)
    halos = []
    for i, edge in enumerate(edges):
        halos.append(to_neighbour(edge, 1 if i % 2 == 0 else -1, i >= 2))
    extended = jnp.concatenate([halos[0], own, halos[1]], axis=0)
    past = jnp.concatenate([halos[2], past, halos[3]], axis=0)
    outgoing = jnp.where(place == lax.axis_size("role") - 1, past, extended)
    one_back = around(outgoing, "role", 1)
    two_back = around(outgoing, "role", 2)
    two_back = jnp.where(place == 0, past, two_back)
    decoded = convolve(extended, one_back, two_back, conv_weight, latent, conv_bias)
    return decoded


def body(
    queries,
    keys,
    values,
    q_gain,
    k_gain,
    latent_frames,
    frame_cache,
    vae_gain,
    conv_weight,
    conv_bias,
):
    width = queries.shape[2]
    ring = lax.axis_size("seq")
    chunks = chunks_of(width // HEAD_DIM, ring)
    early = min(EARLY, len(chunks))
    place = lax.axis_index("seq").astype(jnp.int32)[None]

    first_v = split(place, values[0], ring, chunks[:early])
    v_arrays = [first_v[0]]
    v_arrays += [swap(first_v[mask], "seq", mask) for mask in range(1, ring)]
    decoded = decode(latent_frames, frame_cache, vae_gain, conv_weight, conv_bias)
    packed = pack(
        place, queries[0], keys[0], values[0], q_gain, k_gain, ring, chunks, early
    )
    ready = []
    for index, (near, far) in enumerate(packed):
        span = chunks[index][0]
        near_in = [swap(near[mask], "seq", mask) for mask in range(1, span)]
        far_in = [swap(far[mask % span], "seq", mask) for mask in range(span, ring)]
        ready.append((near[0], far[0], near_in, far_in))
    whole, v_head, pieces, where = None, 0, [], []
    for index, chunk in enumerate(chunks):
        whole, *mixed = attend(
            place,
            chunk,
            ready[index],
            v_arrays if index < early else None,
            v_head,
            whole,
            width,
            RESIDENT and index >= early and chunk[1] < chunks[early][1],
        )
        v_head += chunk[1]
        for mask in range(1, chunk[0]):
            pieces.append(swap(mixed[mask - 1], "seq", mask))
            where.append((mask, chunk))
    final = [
        i
        for i, (mask, chunk) in enumerate(where)
        if chunk == chunks[-1] or (chunk == chunks[0] and mask >= ring // 2)
    ]
    first = [i for i in range(len(where)) if i not in final]
    whole = join(place, [pieces[i] for i in first], [where[i] for i in first], whole)
    attended = join(place, [pieces[i] for i in final], [where[i] for i in final], whole)[None]
    return (attended, decoded[None])


def solution(mesh):
    tokens = P(("groups", "role"), "seq", None)
    frames = P(("groups", "role"), "seq", None, None)
    return jax.shard_map(
        body,
        mesh=mesh,
        in_specs=(
            tokens,
            tokens,
            tokens,
            P(),
            P(),
            frames,
            P("groups", "seq", None, None),
            P(),
            P(),
            P(),
        ),
        out_specs=(tokens, frames),
        check_vma=False,
    )
```
